128 devices in a mesh: seq: 16 (over x, y), head: 8 (over z, core).
Axes of the slice: x: 4, y: 4, z: 4, core: 2. Of those that a mesh axis runs over, the one named last changes fastest.
Arguments:
- query_rows: bfloat16 [65536, 2048], P(('seq', 'head')), may hold values from -6 to 6
- key_rows: bfloat16 [65536, 2048], P(('seq', 'head')), may hold values from -6 to 6
- value_rows: bfloat16 [65536, 2048], P(('seq', 'head')), may hold values from -6 to 6
- gate_rows: bfloat16 [65536, 2048], P(('seq', 'head')), may hold values from -6 to 6
- segment_ids: int32 [512], P('seq'), may hold values from 0 to 3, as said below
- decay_rates: float32 [16], replicated, may hold values from 7.6293946e-07 to 0.00030517578
- norm_gain: float32 [2048], replicated, may hold values from 0.25 to 1.75
- out_weight: bfloat16 [2048, 2048], P(('seq', 'head')), may hold values from -0.125 to 0.125
Outputs:
- mixed_out: bfloat16 [65536, 2048], P(('seq', 'head'))
The draws below stay inside these ranges and needn't reach their ends.
Inputs may be any that keep to these rules, and one draw needn't show every extreme that they name: segment_ids never falls from one block to the next; every document number appears, each document spans 1 to 256 blocks and one spans exactly 256.
All inputs are finite; a program needn't handle non-finite values.
Results may differ from the reference program's by a relative error of at most 0.006.
Values may be sent and summed in bfloat16 or wider, within the bound.
A program may use at most 256 MiB of HBM per device.

```python
import math
import jax
import jax.numpy as jnp
from jax import lax

D = 2048
H = 16
DH = 128
BLK = 128
SBLK = 512
TOKENS = 65536
NBLK = 512
MOST = 256


def draw_segment_ids(key, part):
    key_cuts = jax.random.fold_in(key, 11)
    key_place = jax.random.fold_in(key, 23)
    remain = NBLK - MOST
    picked = jax.random.permutation(key_cuts, remain - 1)[:2] + 1
    cut_low = jnp.minimum(picked[0], picked[1])
    cut_high = jnp.maximum(picked[0], picked[1])
    shorter = jnp.stack([cut_low, cut_high - cut_low, remain - cut_high]).astype(jnp.int32)
    long_place = jax.random.randint(key_place, (), 0, 4)
    slots = jnp.arange(4)
    lower_pick = shorter[jnp.clip(slots, 0, 2)]
    upper_pick = shorter[jnp.clip(slots - 1, 0, 2)]
    lengths = jnp.where(slots < long_place, lower_pick, jnp.where(slots == long_place, MOST, upper_pick)).astype(jnp.int32)
    ends = jnp.cumsum(lengths)
    blocks = jnp.arange(NBLK, dtype=jnp.int32)
    ids = (blocks[:, None] >= ends[None, :3]).astype(jnp.int32).sum(axis=1)
    return ids.astype(jnp.int32)


def level_of(own_key, dims, cuts, low, high):
    def one(axis_at, blocks):
        heights = jax.random.uniform(jax.random.fold_in(jax.random.fold_in(own_key, 6), axis_at), (blocks,), jnp.float32, low / len(cuts), high / len(cuts))
        return jnp.repeat(jnp.exp(heights), dims[axis_at] // blocks).reshape((-1,) + (1,) * (len(dims) - axis_at - 1))

    level = one(*cuts[0])
    for cut in cuts[1:]:
        level = level * one(*cut)
    return level


def scatter_about(rng, extent, deviation, bound, pieces=(), kind=jnp.bfloat16):
    entries = deviation * jax.random.normal(rng, extent, jnp.float32)
    if pieces:
        entries = entries * level_of(rng, extent, pieces, -0.22, 0.18)
    return jnp.clip(entries, -bound, bound).astype(kind)


def setup_inputs(seed: int = 0) -> dict:
    keys = jax.random.split(jax.random.key(seed), 9)
    query_rows = scatter_about(keys[0], (TOKENS, D), 1.0, 6.0, ((0, 128),))
    key_rows = scatter_about(keys[1], (TOKENS, D), 1.0, 6.0, ((0, 128),))
    value_rows = scatter_about(keys[2], (TOKENS, D), 1.0, 6.0, ((0, 128),))
    gate_rows = scatter_about(keys[3], (TOKENS, D), 1.0, 6.0, ((0, 128),))
    segment_ids = draw_segment_ids(jax.random.fold_in(keys[8], 71), 0)
    decay_rates = jnp.clip(jnp.exp(jax.random.uniform(keys[5], (H,), jnp.float32, math.log(7.629394644936838e-07), math.log(0.00030517578))), 7.629394644936838e-07, 0.00030517578)
    norm_gain = jnp.clip(1.0 + 0.15 * jax.random.normal(keys[6], (D,), jnp.float32), 0.25, 1.75)
    out_weight = scatter_about(keys[7], (D, D), D ** -0.5, 0.125, ((0, 128),))
    return {"query_rows": query_rows, "key_rows": key_rows, "value_rows": value_rows, "gate_rows": gate_rows, "segment_ids": segment_ids, "decay_rates": decay_rates, "norm_gain": norm_gain, "out_weight": out_weight}


highest = lax.Precision.HIGHEST

def head_attention(inputs, tok_seg):
    query_head, key_head, value_head, rate_head = inputs
    query_parts = query_head.astype(jnp.float32).reshape(-1, SBLK, DH)
    key_parts = key_head.astype(jnp.float32).reshape(-1, SBLK, DH)
    value_parts = value_head.astype(jnp.float32).reshape(-1, SBLK, DH)
    seg_parts = tok_seg.reshape(-1, SBLK)
    positions = jnp.arange(SBLK, dtype=jnp.float32)
    offsets = positions[:, None] - positions[None, :]
    causal = offsets >= 0

    def advance(carried, blocks_in):
        state_now, prev_seg = carried
        query_part, key_part, value_part, seg_part = blocks_in
        same_doc = (seg_part[:, None] == seg_part[None, :]) & causal
        decay_now = jnp.where(same_doc, jnp.exp(-rate_head * jnp.maximum(offsets, 0.0)), 0.0)
        scores = jnp.dot(query_part, key_part.T, precision=highest)
        rounded = lax.optimization_barrier((scores * decay_now).astype(jnp.bfloat16))
        weights = rounded.astype(jnp.float32)
        inner_part = jnp.dot(weights, value_part, precision=highest)
        reach_row = jnp.where(seg_part == prev_seg, jnp.exp(-rate_head * (positions + 1.0)), 0.0)
        outer_part = reach_row[:, None] * jnp.dot(query_part, state_now, precision=highest)
        last_seg = seg_part[-1]
        keep_row = jnp.where(seg_part == last_seg, jnp.exp(-rate_head * (SBLK - 1.0 - positions)), 0.0)
        carry_keep = jnp.where(last_seg == prev_seg, jnp.exp(-rate_head * SBLK), 0.0)
        new_state = carry_keep * state_now + jnp.dot((key_part * keep_row[:, None]).T, value_part, precision=highest)
        return ((new_state, last_seg), inner_part + outer_part)
    start = (jnp.zeros((DH, DH), jnp.float32), jnp.array(-1.0, jnp.float32))
    ignored, outputs = lax.scan(advance, start, (query_parts, key_parts, value_parts, seg_parts))
    return outputs.reshape(TOKENS, DH).astype(jnp.bfloat16)

def reference(query_rows, key_rows, value_rows, gate_rows, segment_ids, decay_rates, norm_gain, out_weight):
    tok_seg = jnp.repeat(segment_ids, BLK).astype(jnp.float32)
    query_heads = query_rows.reshape(TOKENS, H, DH).transpose(1, 0, 2)
    key_heads = key_rows.reshape(TOKENS, H, DH).transpose(1, 0, 2)
    value_heads = value_rows.reshape(TOKENS, H, DH).transpose(1, 0, 2)
    attention = lax.map(lambda inputs: head_attention(inputs, tok_seg), (query_heads, key_heads, value_heads, decay_rates))
    widened = attention.astype(jnp.float32)
    inv_rms = lax.rsqrt(lax.optimization_barrier(jnp.mean(widened * widened, axis=-1, keepdims=True)) + 1e-06)
    normed = (widened * inv_rms).transpose(1, 0, 2).reshape(TOKENS, D)
    normed = (normed * norm_gain * jax.nn.silu(gate_rows.astype(jnp.float32))).astype(jnp.bfloat16)
    return jnp.dot(normed, out_weight, preferred_element_type=jnp.float32).astype(jnp.bfloat16)
```

```python
import functools

import jax
import jax.numpy as jnp
from jax import lax
from jax.experimental import pallas as pl
from jax.experimental.pallas import tpu as pltpu
from jax.sharding import Mesh
from jax.sharding import PartitionSpec as P

BLK = 128
SBLK = 512
DH = 128
FAR = 1e30
X, Y, Z, C = "seq_0", "seq_1", "head_0", "head_1"
SEQ_HEAD = (X, Y, Z, C)
SEQ = (X, Y)
MESH_ID = pl.DeviceIdType.MESH
F32, BF16 = jnp.float32, jnp.bfloat16

COLOURS = (
    (0, 768, (2, 1, 0)),
    (768, 640, (1, 0, 2)),
    (1408, 640, (0, 2, 1)),
)


def dot(a, b, ca, cb):
    return lax.dot_general(a, b, (((ca,), (cb,)), ((), ())), preferred_element_type=F32)


def same(a, b, n):
    return jnp.where(a == b, n, FAR)


def decay(rate, n):
    return jnp.exp(-rate * jnp.broadcast_to(n, (1, DH)))


def scan_kernel(
    ids, rates, q_hbm, k_hbm, v_hbm, g_hbm, gain, w_in,
    nrm_hbm, w_all,
    q, k, v, g, wbuf, nrm, inner, gated, offs0, offs1, keep_n, reach_n,
    s_own, s_out, s_in, z_out, z_in, p_part, y_out, y_in, x_out, x_in, p_out, p_in, c_out, c_in, p_own,
    load_sem, store_sem, c_send, c_recv, z_send, z_recv, y_send, y_recv, x_send, x_recv,
    p_send, p_recv, d_send, d_recv, w_send, w_recv, b_send, b_recv,
):
    at = (lax.axis_index(X), lax.axis_index(Y), lax.axis_index(Z))
    x, y, z = at
    c = lax.axis_index(C)
    names = (X, Y, Z)

    def near(axis, step):
        return lax.rem(at[axis] + step, 4)

    barrier = pltpu.get_barrier_semaphore()
    pl.semaphore_signal(barrier, inc=1, device_id={C: 1 - c}, device_id_type=MESH_ID)
    for axis in range(3):
        for step in (1, 2, 3):
            pl.semaphore_signal(
                barrier, inc=1, device_id={names[axis]: near(axis, step)}, device_id_type=MESH_ID
            )
    loads = [
        pltpu.make_async_copy(src, dst, load_sem.at[n])
        for n, (src, dst) in enumerate(
            ((k_hbm, k), (v_hbm, v), (w_in, wbuf), (q_hbm, q), (g_hbm, g))
        )
    ]
    for load in loads:
        load.start()

    place = z * 2 + c
    own_id = [ids[place * 4 + b] for b in range(4)]
    row = lax.broadcasted_iota(jnp.int32, (BLK, BLK), 0)
    column = lax.broadcasted_iota(jnp.int32, (BLK, BLK), 1)
    rows = row.astype(F32)
    ahead = (row - column).astype(F32)
    for bi in range(4):
        part = slice(bi * BLK, bi * BLK + BLK)
        keep_n[part, :] = (SBLK - 1.0 - bi * BLK) - rows + same(own_id[bi], own_id[3], 0.0)
        reach_n[part, :] = (1.0 + bi * BLK) + rows + same(own_id[bi], own_id[0], 0.0)
        for bj in range(4):
            if bj >= 2 and bi < 2:
                continue
            if bj > bi:
                block = jnp.full((BLK, BLK), FAR, F32)
            else:
                block = ahead + float(BLK * (bi - bj))
                if bi == bj:
                    block = jnp.where(ahead >= 0, block, FAR)
                block = block + same(own_id[bi], own_id[bj], 0.0)
            if bj < 2:
                offs0[part, bj * BLK : bj * BLK + BLK] = block
            else:
                offs1[bi * BLK - 256 : bi * BLK - 128, bj * BLK - 256 : bj * BLK - 128] = block

    def cols(h):
        return pl.ds(pl.multiple_of(h * DH, DH), DH)

    def states(into, first):
        @pl.loop(0, 8)
        def _(i):
            h = first + i
            kept = k[:, cols(h)].astype(F32) * jnp.exp(-rates[h] * keep_n[...])
            into[i] = dot(kept.astype(BF16), v[:, cols(h)], 0, 0)

    def attend(low, high):
        @pl.loop(low, high)
        def _(h):
            rate = rates[h]
            queries, keys, values = q[:, cols(h)], k[:, cols(h)], v[:, cols(h)]
            scores = dot(queries, keys[:256], 1, 1)
            weights = (scores * jnp.exp(-rate * offs0[...])).astype(BF16)
            total = dot(weights, values[:256], 1, 0)
            scores = dot(queries[256:], keys[256:], 1, 1)
            weights = (scores * jnp.exp(-rate * offs1[...])).astype(BF16)
            inner[h, :256, :] = total[:256]
            inner[h, 256:, :] = total[256:] + dot(weights, values[256:], 1, 0)
            gate = g[:, cols(h)].astype(F32)
            gated[h] = gain[:, cols(h)] * (gate / (1.0 + jnp.exp(-gate)))

    def remote(src, dst, send, recv, to):
        return pltpu.make_async_remote_copy(
            src_ref=src, dst_ref=dst, send_sem=send, recv_sem=recv, device_id=to, device_id_type=MESH_ID
        )

    def piece(colour, phase, coord, half):
        low, wide, order = COLOURS[colour]
        index = list(at) + [c]
        for axis in order[:phase]:
            index[axis] = slice(0, 4)
        index[order[phase]] = coord
        lanes = slice(low, low + wide)
        if half is not None:
            if phase == 0:
                cut = 384
                lanes = slice(low, low + cut) if half == 0 else slice(low + cut, low + wide)
            else:
                index[order[0]] = slice(2 * half, 2 * half + 2)
        return tuple(index) + (slice(None), lanes)

    started = []

    def ring_copy(colour, phase, slot, step, coord, half):
        axis = COLOURS[colour][2][phase]
        where = piece(colour, phase, coord, half)
        src = w_all.at[where]
        if phase == 0 and slot < 4:
            src = wbuf.at[where[-2:]]
        return remote(
            src, w_all.at[where], w_send.at[colour, phase, slot], w_recv.at[colour, phase, slot],
            {names[axis]: near(axis, step)},
        )

    SLOTS = ((1, 0), (1, 1), (3, 1), (3, 0), (1, 0), (3, 1))

    def ring_start(phase):
        for colour in range(3):
            mine = at[COLOURS[colour][2][phase]]
            for slot in (0, 2, 1, 3):
                step, half = SLOTS[slot]
                copy = ring_copy(colour, phase, slot, step, mine, half)
                copy.start()
                started.append(copy)

    def ring_pass(phase):
        for colour in range(3):
            axis = COLOURS[colour][2][phase]
            for slot in (0, 2):
                step, half = SLOTS[slot]
                from_coord = near(axis, 4 - step)
                ring_copy(colour, phase, slot, step, from_coord, half).wait_recv()
                copy = ring_copy(colour, phase, slot + 4 if slot == 0 else 5, step, from_coord, half)
                copy.start()
                started.append(copy)

    def twin_copy(where, slot):
        return remote(w_all.at[where], w_all.at[where], b_send.at[slot], b_recv.at[slot], {C: 1 - c})

    def other(where):
        return where[:3] + (1 - c,) + where[4:]

    twins = []

    def twin(where, slot):
        copy = twin_copy(where, slot)
        copy.start()
        started.append(copy)
        twins.append((other(where), slot))

    def ring_end(phase):
        for colour in range(3):
            axis = COLOURS[colour][2][phase]
            for slot in (1, 3):
                step, half = SLOTS[slot]
                ring_copy(colour, phase, slot, step, near(axis, 4 - step), half).wait_recv()
            base = (colour * 3 + phase) * 3
            twin(piece(colour, phase, near(axis, 1), None), base)
            twin(piece(colour, phase, near(axis, 3), None), base + 1)
        for colour in range(3):
            axis = COLOURS[colour][2][phase]
            for slot in (4, 5):
                step, half = SLOTS[slot]
                ring_copy(colour, phase, slot, step, near(axis, 2), half).wait_recv()
            twin(piece(colour, phase, near(axis, 2), None), (colour * 3 + phase) * 3 + 2)

    loads[0].wait()
    loads[1].wait()
    states(s_out, (1 - c) * 8)
    pl.semaphore_wait(barrier, 10)
    core_copy = remote(s_out, s_in, c_send, c_recv, {C: 1 - c})
    core_copy.start()
    loads[2].wait()
    ring_start(0)
    own_store = pltpu.make_async_copy(wbuf, w_all.at[x, y, z, c], store_sem.at[2])
    own_store.start()
    states(s_own, c * 8)
    core_copy.wait()

    chip = z * 8
    n_first = jnp.where(c == 0, same(ids[chip + 3], ids[chip + 7], 512.0), 0.0)
    n_second = jnp.where(c == 1, same(ids[chip + 3], ids[chip + 7], 512.0), 0.0)
    for i in range(8):
        rate = rates[c * 8 + i]
        both = s_own[i] * decay(rate, n_first) + s_in[i] * decay(rate, n_second)
        z_out[i // 2, (i % 2) * DH : (i % 2) * DH + DH, :] = both.astype(BF16)
    line_copies = []
    for step in (1, 3, 2):
        to = near(2, step)
        copy = remote(z_out.at[to], z_in.at[3 - step], z_send.at[step - 1], z_recv.at[3 - step], {Z: to})
        copy.start()
        line_copies.append(copy)
    loads[3].wait()
    loads[4].wait()
    ring_pass(0)
    attend(0, 2)
    for copy in line_copies:
        copy.wait()

    two = [rates[c * 8 + z * 2 + j] for j in range(2)]
    spots = [near(2, step) for step in range(4)]
    line_last = ids[31]

    def held(step, j):
        part = slice(j * DH, j * DH + DH)
        block = z_out[z, part, :] if step == 0 else z_in[step - 1, part, :]
        return block.astype(F32)

    for j in range(2):
        total = None
        for step in range(4):
            spot = spots[step]
            n = same(ids[spot * 8 + 7], line_last, (1024 * (3 - spot)).astype(F32))
            term = held(step, j) * decay(two[j], n)
            total = term if total is None else total + term
        y_out[j * DH : j * DH + DH, :] = total
    y_out[2 * DH : 2 * DH + 8, :] = jnp.broadcast_to(line_last.astype(F32), (8, DH))
    column_copies = []
    for step in (1, 3, 2):
        copy = remote(
            y_out, y_in.at[3 - step], y_send.at[step - 1], y_recv.at[3 - step], {Y: near(1, step)}
        )
        copy.start()
        column_copies.append(copy)
    own_store.wait()
    twin((x, y, z, c, slice(None), slice(None)), 27)
    ring_end(0)
    ring_start(1)
    for t in range(4):
        target = spots[t]
        for j in range(2):
            total = None
            for step in range(4):
                if step == t:
                    continue
                spot = spots[step]
                n = same(ids[spot * 8 + 7], ids[target * 8], (1024 * (target - 1 - spot)).astype(F32))
                term = held(step, j) * decay(two[j], jnp.where(spot < target, n, FAR))
                total = term if total is None else total + term
            p_part[t, j * DH : j * DH + DH, :] = total
    attend(2, 4)
    for copy in column_copies:
        copy.wait()

    def gathered(own, came, step):
        return own if step == 0 else came.at[step - 1]

    def note(ref):
        return ref[2 * DH : 2 * DH + 1, :]

    line_first = ids[0].astype(F32)
    spots_y = [near(1, step) for step in range(4)]
    last_note = jnp.zeros((1, DH), F32)
    for step in range(4):
        last_note = last_note + jnp.where(spots_y[step] == 3, 1.0, 0.0) * note(gathered(y_out, y_in, step))
    for j in range(2):
        part = slice(j * DH, j * DH + DH)
        total = None
        for step in range(4):
            ref, spot = gathered(y_out, y_in, step), spots_y[step]
            n = same(note(ref), last_note, (4096 * (3 - spot)).astype(F32))
            term = ref[part, :] * decay(two[j], n)
            total = term if total is None else total + term
        x_out[part, :] = total
    x_out[2 * DH : 2 * DH + 8, :] = jnp.broadcast_to(last_note, (8, DH))
    slab_copies = []
    for step in (1, 3, 2):
        copy = remote(
            x_out, x_in.at[3 - step], x_send.at[step - 1], x_recv.at[3 - step], {X: near(0, step)}
        )
        copy.start()
        slab_copies.append(copy)
    ring_pass(1)
    attend(4, 7)
    ring_end(1)
    ring_start(2)
    for copy in slab_copies:
        copy.wait()

    spots_x = [near(0, step) for step in range(4)]
    for j in range(2):
        part = slice(j * DH, j * DH + DH)
        total = jnp.zeros((DH, DH), F32)
        for step in range(1, 4):
            ref, spot = y_in.at[step - 1], spots_y[step]
            n = same(note(ref), line_first, (4096 * (y - 1 - spot)).astype(F32))
            total = total + ref[part, :] * decay(two[j], jnp.where(spot < y, n, FAR))
            ref, spot = x_in.at[step - 1], spots_x[step]
            n = same(note(ref), line_first, (16384 * (x - 1 - spot) + 4096 * y).astype(F32))
            total = total + ref[part, :] * decay(two[j], jnp.where(spot < x, n, FAR))
        for t in range(4):
            target = spots[t]
            n = same(ids[0], ids[target * 8], (1024 * target).astype(F32))
            p_out[t, part, :] = (p_part[t, part, :] + total * decay(two[j], n)).astype(BF16)
    back_copies = []
    for step in (1, 3, 2):
        copy = remote(
            p_out.at[step], p_in.at[3 - step], p_send.at[step - 1], p_recv.at[3 - step], {Z: near(2, step)}
        )
        copy.start()
        back_copies.append(copy)
    attend(7, 12)
    ring_pass(2)
    for copy in back_copies:
        copy.wait()

    n_chip = same(ids[chip], ids[chip + 4], 512.0)
    n_core = same(ids[chip + 3], ids[chip + 4], 0.0)
    mine = jnp.where(c == 1, n_core, FAR)
    theirs = jnp.where(c == 0, n_core, FAR)
    for step in range(4):
        for j in range(2):
            i = spots[step] * 2 + j
            rate = rates[c * 8 + i]
            part = slice(j * DH, j * DH + DH)
            before = (p_out[0, part, :] if step == 0 else p_in[step - 1, part, :]).astype(F32)
            own = before * decay(rate, jnp.where(c == 1, n_chip, 0.0)) + s_in[i] * decay(rate, mine)
            away = before * decay(rate, jnp.where(c == 0, n_chip, 0.0)) + s_own[i] * decay(rate, theirs)
            p_own[i] = own.astype(BF16)
            c_out[i] = away.astype(BF16)
    pair_copy = remote(c_out, c_in, d_send, d_recv, {C: 1 - c})
    pair_copy.start()
    attend(12, 16)

    def finish(first, ref):
        @pl.loop(0, 8)
        def _(i):
            h = first + i
            carried = dot(q[:, cols(h)], ref[i], 1, 0)
            mixed = inner[h] + carried * jnp.exp(-rates[h] * reach_n[...])
            mixed = mixed.astype(BF16).astype(F32)
            inv = lax.rsqrt(jnp.mean(mixed * mixed, axis=-1, keepdims=True) + 1e-06)
            nrm[:, cols(h)] = (mixed * inv * gated[h]).astype(BF16)

    def put(first, slot):
        half = pl.ds(pl.multiple_of(first * DH, 1024), 1024)
        return pltpu.make_async_copy(nrm.at[:, half], nrm_hbm.at[:, half], store_sem.at[slot])

    finish(c * 8, p_own)
    put(c * 8, 0).start()
    pair_copy.wait()
    finish((1 - c) * 8, c_in)
    put((1 - c) * 8, 1).start()

    ring_end(2)
    for where, slot in twins:
        twin_copy(where, slot).wait_recv()
    for copy in started:
        copy.wait_send()
    put(c * 8, 0).wait()
    put((1 - c) * 8, 1).wait()


def gather_and_attend(ids, rates, q, k, v, g, gain, w):
    tokens, width = q.shape
    heads = rates.shape[0]
    hbm = pl.BlockSpec(memory_space=pl.ANY)
    smem = pl.BlockSpec(memory_space=pltpu.SMEM)
    vmem = pltpu.VMEM
    dma = pltpu.SemaphoreType.DMA
    rows = w.shape[0]
    return pl.pallas_call(
        scan_kernel,
        out_shape=(
            jax.ShapeDtypeStruct((tokens, width), BF16),
            jax.ShapeDtypeStruct((4, 4, 4, 2, rows, width), BF16),
        ),
        in_specs=[smem, smem, hbm, hbm, hbm, hbm, pl.BlockSpec(memory_space=vmem), hbm],
        out_specs=(hbm, hbm),
        scratch_shapes=[
            vmem((tokens, width), BF16),
            vmem((tokens, width), BF16),
            vmem((tokens, width), BF16),
            vmem((tokens, width), BF16),
            vmem((rows, width), BF16),
            vmem((tokens, width), BF16),
            vmem((heads, tokens, DH), F32),
            vmem((heads, tokens, DH), F32),
            vmem((512, 256), F32),
            vmem((256, 256), F32),
            vmem((512, DH), F32),
            vmem((512, DH), F32),
            vmem((8, DH, DH), F32),
            vmem((8, DH, DH), F32),
            vmem((8, DH, DH), F32),
            vmem((4, 2 * DH, DH), BF16),
            vmem((3, 2 * DH, DH), BF16),
            vmem((4, 2 * DH, DH), F32),
            vmem((2 * DH + 8, DH), F32),
            vmem((3, 2 * DH + 8, DH), F32),
            vmem((2 * DH + 8, DH), F32),
            vmem((3, 2 * DH + 8, DH), F32),
            vmem((4, 2 * DH, DH), BF16),
            vmem((3, 2 * DH, DH), BF16),
            vmem((8, DH, DH), BF16),
            vmem((8, DH, DH), BF16),
            vmem((8, DH, DH), BF16),
            dma((5,)),
            dma((3,)),
            dma, dma,
            dma((3,)), dma((3,)),
            dma((3,)), dma((3,)),
            dma((3,)), dma((3,)),
            dma((3,)), dma((3,)),
            dma, dma,
            dma((3, 3, 6)), dma((3, 3, 6)),
            dma((28,)), dma((28,)),
        ],
        compiler_params=pltpu.CompilerParams(
            collective_id=0, has_side_effects=True, vmem_limit_bytes=60 << 20
        ),
        name="scan_and_gather",
    )(ids, rates, q, k, v, g, gain, w)


def on_device(query_rows, key_rows, value_rows, gate_rows, segment_ids, decay_rates, norm_gain, out_weight):
    width = query_rows.shape[1]
    normed, weight = gather_and_attend(
        segment_ids, decay_rates, query_rows, key_rows, value_rows, gate_rows,
        norm_gain.reshape(1, width), out_weight,
    )
    return jnp.dot(
        normed, weight.reshape(width, width), preferred_element_type=F32
    ).astype(BF16)


def solution(mesh):
    split = Mesh(mesh.devices.reshape(4, 4, 4, 2), SEQ_HEAD)
    rows = P(SEQ_HEAD, None)
    return jax.shard_map(
        on_device,
        mesh=split,
        in_specs=(rows, rows, rows, rows, P(SEQ), P(), P(), rows),
        out_specs=rows,
        check_vma=False,
    )
```

```python
import functools

import jax
import jax.numpy as jnp
from jax import lax
from jax.experimental import pallas as pl
from jax.experimental.pallas import tpu as pltpu
from jax.sharding import Mesh
from jax.sharding import PartitionSpec as P

BLK = 128
SBLK = 512
DH = 128
FAR = 1e30
X, Y, Z, C = "seq_0", "seq_1", "head_0", "head_1"
SEQ_HEAD = (X, Y, Z, C)
SEQ = (X, Y)
MESH_ID = pl.DeviceIdType.MESH
F32, BF16 = jnp.float32, jnp.bfloat16

COLOURS = (
    (0, 768, (2, 1, 0)),
    (768, 640, (1, 0, 2)),
    (1408, 640, (0, 2, 1)),
)


def dot(a, b, ca, cb):
    return lax.dot_general(a, b, (((ca,), (cb,)), ((), ())), preferred_element_type=F32)


def same(a, b, n):
    return jnp.where(a == b, n, FAR)


def decay(rate, n):
    return jnp.exp(-rate * jnp.broadcast_to(n, (1, DH)))


def scan_kernel(
    ids, rates, q_hbm, k_hbm, v_hbm, g_hbm, gain, w_in,
    nrm_hbm, w_all,
    q, k, v, g, wbuf, nrm, inner, gated, offs0, offs1, keep_n, lasting, reach_n,
    s_own, s_out, s_in, z_out, z_in, p_part, y_out, y_in, x_out, x_in, u_out, u_in, m_out, m_in,
    p_out, p_in, c_out, c_in, p_own,
    load_sem, store_sem, c_send, c_recv, z_send, z_recv, y_send, y_recv, x_send, x_recv,
    u_send, u_recv, m_send, m_recv, p_send, p_recv, d_send, d_recv, w_send, w_recv, b_send, b_recv,
):
    at = (lax.axis_index(X), lax.axis_index(Y), lax.axis_index(Z))
    x, y, z = at
    c = lax.axis_index(C)
    names = (X, Y, Z)

    def near(axis, step):
        return lax.rem(at[axis] + step, 4)

    barrier = pltpu.get_barrier_semaphore()
    pl.semaphore_signal(barrier, inc=1, device_id={C: 1 - c}, device_id_type=MESH_ID)
    for axis in range(3):
        for step in (1, 2, 3):
            pl.semaphore_signal(
                barrier, inc=1, device_id={names[axis]: near(axis, step)}, device_id_type=MESH_ID
            )
    loads = [
        pltpu.make_async_copy(src, dst, load_sem.at[n])
        for n, (src, dst) in enumerate(
            ((w_in, wbuf), (k_hbm, k), (v_hbm, v), (q_hbm, q), (g_hbm, g))
        )
    ]
    for load in loads:
        load.start()

    place = z * 2 + c
    own_id = [ids[place * 4 + b] for b in range(4)]
    row = lax.broadcasted_iota(jnp.int32, (BLK, BLK), 0)
    column = lax.broadcasted_iota(jnp.int32, (BLK, BLK), 1)
    rows = row.astype(F32)
    ahead = (row - column).astype(F32)
    for bi in range(4):
        part = slice(bi * BLK, bi * BLK + BLK)
        keep_n[part, :] = (SBLK - 1.0 - bi * BLK) - rows + same(own_id[bi], own_id[3], 0.0)
        lasting[part, :] = jnp.full((BLK, DH), jnp.where(own_id[bi] == own_id[3], 1.0, 0.0), F32)
        reach_n[part, :] = (1.0 + bi * BLK) + rows + same(own_id[bi], own_id[0], 0.0)
        for bj in range(4):
            if bj >= 2 and bi < 2:
                continue
            if bj > bi:
                block = jnp.full((BLK, BLK), FAR, F32)
            else:
                block = ahead + float(BLK * (bi - bj))
                if bi == bj:
                    block = jnp.where(ahead >= 0, block, FAR)
                block = block + same(own_id[bi], own_id[bj], 0.0)
            if bj < 2:
                offs0[part, bj * BLK : bj * BLK + BLK] = block
            else:
                offs1[bi * BLK - 256 : bi * BLK - 128, bj * BLK - 256 : bj * BLK - 128] = block

    def cols(h):
        return pl.ds(pl.multiple_of(h * DH, DH), DH)

    def states(into, first):
        @pl.loop(0, 8)
        def _(i):
            h = first + i
            keys, values = k[:, cols(h)], v[:, cols(h)]
            lost = keys.astype(F32) * (lasting[...] - jnp.exp(-rates[h] * keep_n[...]))
            exact = keys * lasting[...].astype(BF16)
            into[i] = dot(exact, values, 0, 0) - dot(lost.astype(BF16), values, 0, 0)

    def attend(low, high):
        @pl.loop(low, high)
        def _(h):
            rate = rates[h]
            queries, keys, values = q[:, cols(h)], k[:, cols(h)], v[:, cols(h)]
            scores = dot(queries, keys[:256], 1, 1)
            weights = (scores * jnp.exp(-rate * offs0[...])).astype(BF16)
            total = dot(weights, values[:256], 1, 0)
            scores = dot(queries[256:], keys[256:], 1, 1)
            weights = (scores * jnp.exp(-rate * offs1[...])).astype(BF16)
            inner[h, :256, :] = total[:256]
            inner[h, 256:, :] = total[256:] + dot(weights, values[256:], 1, 0)
            gate = g[:, cols(h)].astype(F32)
            gated[h] = gain[:, cols(h)] * (gate / (1.0 + jnp.exp(-gate)))

    def remote(src, dst, send, recv, to):
        return pltpu.make_async_remote_copy(
            src_ref=src, dst_ref=dst, send_sem=send, recv_sem=recv, device_id=to, device_id_type=MESH_ID
        )

    SLOTS = ((1, 0), (1, 1), (3, 1), (3, 0), (1, 0), (3, 1))

    def phase_of(group):
        return min(group, 2)

    def piece(colour, group, coord, half):
        low, wide, order = COLOURS[colour]
        phase = phase_of(group)
        index = list(at) + [c]
        lanes = slice(low, low + wide)
        if phase == 0:
            if half is not None:
                lanes = slice(low, low + 384) if half == 0 else slice(low + 384, low + wide)
        else:
            index[order[0]] = slice(0, 4) if half is None else slice(2 * half, 2 * half + 2)
        if phase == 2:
            index[order[1]] = near(order[1], group - 2)
        index[order[phase]] = coord
        return tuple(index) + (slice(None), lanes)

    started = []

    def ring_copy(colour, group, slot, step, coord, half):
        axis = COLOURS[colour][2][phase_of(group)]
        where = piece(colour, group, coord, half)
        src = w_all.at[where]
        if group == 0 and slot < 4:
            src = wbuf.at[where[-2:]]
        return remote(
            src, w_all.at[where], w_send.at[colour, group, slot], w_recv.at[colour, group, slot],
            {names[axis]: near(axis, step)},
        )

    def ring_start(group):
        for colour in range(3):
            mine = at[COLOURS[colour][2][phase_of(group)]]
            for slot in (0, 2, 1, 3):
                step, half = SLOTS[slot]
                copy = ring_copy(colour, group, slot, step, mine, half)
                copy.start()
                started.append(copy)

    def ring_pass(group):
        for colour in range(3):
            axis = COLOURS[colour][2][phase_of(group)]
            for slot in (0, 2):
                step, half = SLOTS[slot]
                from_coord = near(axis, 4 - step)
                ring_copy(colour, group, slot, step, from_coord, half).wait_recv()
                copy = ring_copy(colour, group, 4 if slot == 0 else 5, step, from_coord, half)
                copy.start()
                started.append(copy)

    twins = []

    def twin(where, slot):
        copy = remote(w_all.at[where], w_all.at[where], b_send.at[slot], b_recv.at[slot], {C: 1 - c})
        copy.start()
        started.append(copy)
        twins.append((where[:3] + (1 - c,) + where[4:], slot))

    def ring_end(group):
        for colour in range(3):
            axis = COLOURS[colour][2][phase_of(group)]
            for slot in (1, 3):
                step, half = SLOTS[slot]
                ring_copy(colour, group, slot, step, near(axis, 4 - step), half).wait_recv()
            if group > 0:
                twin(piece(colour, group, near(axis, 1), None), 18 * colour + 3 * group)
                twin(piece(colour, group, near(axis, 3), None), 18 * colour + 3 * group + 1)
        for colour in range(3):
            axis = COLOURS[colour][2][phase_of(group)]
            for slot in (4, 5):
                step, half = SLOTS[slot]
                ring_copy(colour, group, slot, step, near(axis, 2), half).wait_recv()
            if group == 0:
                twin(piece(colour, 1, at[COLOURS[colour][2][1]], None), 18 * colour)
            else:
                twin(piece(colour, group, near(axis, 2), None), 18 * colour + 3 * group + 2)

    def twin_waits():
        for where, slot in twins:
            view = w_all.at[where]
            remote(view, view, b_send.at[slot], b_recv.at[slot], {C: 1 - c}).wait_recv()

    pl.semaphore_wait(barrier, 10)
    loads[0].wait()
    ring_start(0)
    own_store = pltpu.make_async_copy(wbuf, w_all.at[x, y, z, c], store_sem.at[2])
    own_store.start()
    loads[1].wait()
    loads[2].wait()
    states(s_out, (1 - c) * 8)
    core_copy = remote(s_out, s_in, c_send, c_recv, {C: 1 - c})
    core_copy.start()
    states(s_own, c * 8)
    core_copy.wait()

    chip = z * 8
    n_first = jnp.where(c == 0, same(ids[chip + 3], ids[chip + 7], 512.0), 0.0)
    n_second = jnp.where(c == 1, same(ids[chip + 3], ids[chip + 7], 512.0), 0.0)
    for i in range(8):
        rate = rates[c * 8 + i]
        both = s_own[i] * decay(rate, n_first) + s_in[i] * decay(rate, n_second)
        z_out[i // 2, (i % 2) * DH : (i % 2) * DH + DH, :] = both.astype(BF16)

    def spread(copies):
        for copy in copies:
            copy.start()
        return copies

    def settle(copies):
        for copy in copies:
            copy.wait()

    line_copies = spread([
        remote(
            z_out.at[near(2, step)], z_in.at[3 - step], z_send.at[step - 1], z_recv.at[3 - step],
            {Z: near(2, step)},
        )
        for step in (1, 3, 2)
    ])
    loads[3].wait()
    loads[4].wait()
    ring_pass(0)
    attend(0, 1)
    own_store.wait()
    ring_end(0)
    ring_start(1)
    ring_start(2)
    attend(1, 4)
    ring_pass(1)
    attend(4, 5)
    settle(line_copies)

    two = [rates[c * 8 + z * 2 + j] for j in range(2)]
    spots = [near(2, step) for step in range(4)]
    line_first, line_last = ids[0], ids[31]
    halves = (slice(0, DH), slice(DH, 2 * DH))

    def held(step, j):
        block = z_out[z, halves[j], :] if step == 0 else z_in[step - 1, halves[j], :]
        return block.astype(F32)

    for j, out in enumerate((y_out, x_out)):
        total = None
        for step in range(4):
            spot = spots[step]
            n = same(ids[spot * 8 + 7], line_last, (1024 * (3 - spot)).astype(F32))
            term = held(step, j) * decay(two[j], n)
            total = term if total is None else total + term
        out[:DH, :] = total.astype(BF16)
        note_row = lax.broadcasted_iota(jnp.int32, (16, DH), 0)
        notes = jnp.where(note_row < 8, line_last.astype(F32), line_first.astype(F32))
        out[DH : DH + 16, :] = notes.astype(BF16)
    column_copies = spread(
        [
            remote(
                src, into.at[3 - step], send.at[step - 1], recv.at[3 - step],
                {names[axis]: near(axis, step)},
            )
            for step in (1, 3, 2)
            for axis, src, into, send, recv in (
                (1, y_out, y_in, y_send, y_recv), (0, x_out, x_in, x_send, x_recv),
            )
        ]
    )
    for t in range(4):
        target = spots[t]
        for j in range(2):
            total = None
            for step in range(4):
                if step == t:
                    continue
                spot = spots[step]
                n = same(ids[spot * 8 + 7], ids[target * 8], (1024 * (target - 1 - spot)).astype(F32))
                term = held(step, j) * decay(two[j], jnp.where(spot < target, n, FAR))
                total = term if total is None else total + term
            p_part[t, halves[j], :] = total
    ring_end(1)
    for group in (3, 5, 4):
        ring_start(group)
    ring_pass(2)
    attend(5, 8)
    settle(column_copies)

    spots_y = [near(1, step) for step in range(4)]
    spots_x = [near(0, step) for step in range(4)]

    def view(own, came, step):
        return own if step == 0 else came.at[step - 1]

    def body_of(ref):
        return ref[:DH, :].astype(F32)

    def last_of(ref):
        return ref[DH : DH + 1, :].astype(F32)

    def first_of(ref):
        return ref[DH + 8 : DH + 9, :].astype(F32)

    by_y = [view(y_out, y_in, step) for step in range(4)]
    by_x = [view(x_out, x_in, step) for step in range(4)]
    slab_last = jnp.zeros((1, DH), F32)
    for step in range(4):
        slab_last = slab_last + jnp.where(spots_y[step] == 3, 1.0, 0.0) * last_of(by_y[step])
    total = None
    for step in range(4):
        spot = spots_y[step]
        n = same(last_of(by_y[step]), slab_last, (4096 * (3 - spot)).astype(F32))
        term = body_of(by_y[step]) * decay(two[0], n)
        total = term if total is None else total + term
    u_out[:DH, :] = total.astype(BF16)
    u_out[DH : DH + 16, :] = jnp.broadcast_to(slab_last, (16, DH)).astype(BF16)
    for t in range(4):
        target, first = spots_y[t], first_of(by_y[t])
        total = None
        for step in range(4):
            ref = by_x[step]
            if step == 0:
                n = same(last_of(ref), first, (4096 * (target - 1 - y)).astype(F32))
                n = jnp.where(y < target, n, FAR)
            else:
                spot = spots_x[step]
                lines = 4 * (x - spot) - y - 1 + target
                n = same(last_of(ref), first, (4096 * lines).astype(F32))
                n = jnp.where(spot < x, n, FAR)
            term = body_of(ref) * decay(two[1], n)
            total = term if total is None else total + term
        m_out[t] = total.astype(BF16)
    slab_copies = spread(
        [
            copy
            for step in (1, 3, 2)
            for copy in (
                remote(
                    u_out, u_in.at[3 - step], u_send.at[step - 1], u_recv.at[3 - step],
                    {X: near(0, step)},
                ),
                remote(
                    m_out.at[step], m_in.at[3 - step], m_send.at[step - 1], m_recv.at[3 - step],
                    {Y: near(1, step)},
                ),
            )
        ]
    )
    attend(8, 9)
    ring_end(2)
    ring_pass(3)
    attend(9, 11)
    settle(slab_copies)

    total = jnp.zeros((DH, DH), F32)
    first = line_first.astype(F32)
    for step in range(1, 4):
        ref, spot = by_y[step], spots_y[step]
        n = same(last_of(ref), first, (4096 * (y - 1 - spot)).astype(F32))
        total = total + body_of(ref) * decay(two[0], jnp.where(spot < y, n, FAR))
        ref, spot = u_in.at[step - 1], spots_x[step]
        n = same(last_of(ref), first, (16384 * (x - 1 - spot) + 4096 * y).astype(F32))
        total = total + body_of(ref) * decay(two[0], jnp.where(spot < x, n, FAR))
    fronts = [total]
    total = m_out[0].astype(F32)
    for step in range(3):
        total = total + m_in[step].astype(F32)
    fronts.append(total)
    for t in range(4):
        n = same(line_first, ids[spots[t] * 8], (1024 * spots[t]).astype(F32))
        for j in range(2):
            whole = p_part[t, halves[j], :] + fronts[j] * decay(two[j], n)
            p_out[t, halves[j], :] = whole.astype(BF16)
    back_copies = spread([
        remote(
            p_out.at[step], p_in.at[3 - step], p_send.at[step - 1], p_recv.at[3 - step],
            {Z: near(2, step)},
        )
        for step in (1, 3, 2)
    ])
    ring_pass(5)
    attend(11, 13)
    ring_pass(4)
    attend(13, 15)
    settle(back_copies)

    n_chip = same(ids[chip], ids[chip + 4], 512.0)
    n_core = same(ids[chip + 3], ids[chip + 4], 0.0)
    mine = jnp.where(c == 1, n_core, FAR)
    theirs = jnp.where(c == 0, n_core, FAR)
    for step in range(4):
        for j in range(2):
            i = spots[step] * 2 + j
            rate = rates[c * 8 + i]
            before = (p_out[0, halves[j], :] if step == 0 else p_in[step - 1, halves[j], :]).astype(F32)
            own = before * decay(rate, jnp.where(c == 1, n_chip, 0.0)) + s_in[i] * decay(rate, mine)
            away = before * decay(rate, jnp.where(c == 0, n_chip, 0.0)) + s_own[i] * decay(rate, theirs)
            p_own[i] = own.astype(BF16)
            c_out[i] = away.astype(BF16)
    pair_copy = remote(c_out, c_in, d_send, d_recv, {C: 1 - c})
    pair_copy.start()
    attend(15, 16)
    ring_end(3)

    def finish(first, ref):
        @pl.loop(0, 8)
        def _(i):
            h = first + i
            carried = dot(q[:, cols(h)], ref[i], 1, 0)
            mixed = inner[h] + carried * jnp.exp(-rates[h] * reach_n[...])
            mixed = mixed.astype(BF16).astype(F32)
            inv = lax.rsqrt(jnp.mean(mixed * mixed, axis=-1, keepdims=True) + 1e-06)
            nrm[:, cols(h)] = (mixed * inv * gated[h]).astype(BF16)

    def put(first, slot):
        half = pl.ds(pl.multiple_of(first * DH, 1024), 1024)
        return pltpu.make_async_copy(nrm.at[:, half], nrm_hbm.at[:, half], store_sem.at[slot])

    finish(c * 8, p_own)
    put(c * 8, 0).start()
    ring_end(5)
    ring_end(4)
    pair_copy.wait()
    finish((1 - c) * 8, c_in)
    put((1 - c) * 8, 1).start()
    twin_waits()
    for copy in started:
        copy.wait_send()
    put(c * 8, 0).wait()
    put((1 - c) * 8, 1).wait()


def gather_and_attend(ids, rates, q, k, v, g, gain, w):
    tokens, width = q.shape
    heads = rates.shape[0]
    hbm = pl.BlockSpec(memory_space=pl.ANY)
    smem = pl.BlockSpec(memory_space=pltpu.SMEM)
    vmem = pltpu.VMEM
    dma = pltpu.SemaphoreType.DMA
    rows = w.shape[0]
    return pl.pallas_call(
        scan_kernel,
        out_shape=(
            jax.ShapeDtypeStruct((tokens, width), BF16),
            jax.ShapeDtypeStruct((4, 4, 4, 2, rows, width), BF16),
        ),
        in_specs=[smem, smem, hbm, hbm, hbm, hbm, pl.BlockSpec(memory_space=vmem), hbm],
        out_specs=(hbm, hbm),
        scratch_shapes=[
            vmem((tokens, width), BF16),
            vmem((tokens, width), BF16),
            vmem((tokens, width), BF16),
            vmem((tokens, width), BF16),
            vmem((rows, width), BF16),
            vmem((tokens, width), BF16),
            vmem((heads, tokens, DH), F32),
            vmem((heads, tokens, DH), F32),
            vmem((512, 256), F32),
            vmem((256, 256), F32),
            vmem((512, DH), F32),
            vmem((512, DH), F32),
            vmem((512, DH), F32),
            vmem((8, DH, DH), F32),
            vmem((8, DH, DH), F32),
            vmem((8, DH, DH), F32),
            vmem((4, 2 * DH, DH), BF16),
            vmem((3, 2 * DH, DH), BF16),
            vmem((4, 2 * DH, DH), F32),
            vmem((DH + 16, DH), BF16),
            vmem((3, DH + 16, DH), BF16),
            vmem((DH + 16, DH), BF16),
            vmem((3, DH + 16, DH), BF16),
            vmem((DH + 16, DH), BF16),
            vmem((3, DH + 16, DH), BF16),
            vmem((4, DH, DH), BF16),
            vmem((3, DH, DH), BF16),
            vmem((4, 2 * DH, DH), BF16),
            vmem((3, 2 * DH, DH), BF16),
            vmem((8, DH, DH), BF16),
            vmem((8, DH, DH), BF16),
            vmem((8, DH, DH), BF16),
            dma((5,)),
            dma((3,)),
            dma, dma,
            dma((3,)), dma((3,)),
            dma((3,)), dma((3,)),
            dma((3,)), dma((3,)),
            dma((3,)), dma((3,)),
            dma((3,)), dma((3,)),
            dma((3,)), dma((3,)),
            dma, dma,
            dma((3, 6, 6)), dma((3, 6, 6)),
            dma((54,)), dma((54,)),
        ],
        compiler_params=pltpu.CompilerParams(
            collective_id=0, has_side_effects=True, vmem_limit_bytes=60 << 20
        ),
        name="scan_and_gather",
    )(ids, rates, q, k, v, g, gain, w)


def project_kernel(a, b, o):
    o[...] = jnp.dot(a[...], b[...], preferred_element_type=F32).astype(BF16)


def project(a, b):
    rows, depth = a.shape
    columns = b.shape[1]
    tile = 1024
    return pl.pallas_call(
        project_kernel,
        out_shape=jax.ShapeDtypeStruct((rows, columns), BF16),
        grid=(columns // tile,),
        in_specs=[
            pl.BlockSpec((rows, depth), lambda j: (0, 0)),
            pl.BlockSpec((depth, tile), lambda j: (0, j)),
        ],
        out_specs=pl.BlockSpec((rows, tile), lambda j: (0, j)),
        compiler_params=pltpu.CompilerParams(vmem_limit_bytes=60 << 20),
        name="project",
    )(a, b)


def on_device(query_rows, key_rows, value_rows, gate_rows, segment_ids, decay_rates, norm_gain, out_weight):
    width = query_rows.shape[1]
    normed, weight = gather_and_attend(
        segment_ids, decay_rates, query_rows, key_rows, value_rows, gate_rows,
        norm_gain.reshape(1, width), out_weight,
    )
    return project(normed, weight.reshape(width, width))


def solution(mesh):
    split = Mesh(mesh.devices.reshape(4, 4, 4, 2), SEQ_HEAD)
    rows = P(SEQ_HEAD, None)
    return jax.shard_map(
        on_device,
        mesh=split,
        in_specs=(rows, rows, rows, rows, P(SEQ), P(), P(), rows),
        out_specs=rows,
        check_vma=False,
    )
```

```python
import functools

import jax
import jax.numpy as jnp
from jax import lax
from jax.experimental import pallas as pl
from jax.experimental.pallas import tpu as pltpu
from jax.sharding import Mesh
from jax.sharding import PartitionSpec as P

BLK = 128
SBLK = 512
DH = 128
FAR = 1e30
X, Y, Z, C = "seq_0", "seq_1", "head_0", "head_1"
SEQ_HEAD = (X, Y, Z, C)
SEQ = (X, Y)
MESH_ID = pl.DeviceIdType.MESH
F32, BF16 = jnp.float32, jnp.bfloat16

COLOURS = (
    (0, 768, (2, 1, 0)),
    (768, 640, (1, 0, 2)),
    (1408, 640, (0, 2, 1)),
)


def dot(a, b, ca, cb):
    return lax.dot_general(a, b, (((ca,), (cb,)), ((), ())), preferred_element_type=F32)


def same(a, b, n):
    return jnp.where(a == b, n, FAR)


def decay(rate, n):
    return jnp.exp(-rate * jnp.broadcast_to(n, (1, DH)))


def scan_kernel(
    ids, rates, q_hbm, k_hbm, v_hbm, g_hbm, gain, w_in,
    nrm_hbm, w_all,
    q, k, v, g, wbuf, nrm, inner, gated, keep_n, lasting,
    s_own, s_out, s_in, z_out, z_in, p_part, y_out, y_in, x_out, x_in, u_out, u_in, m_out, m_in,
    p_out, p_in, c_out, c_in, p_own,
    load_sem, store_sem, c_send, c_recv, z_send, z_recv, y_send, y_recv, x_send, x_recv,
    u_send, u_recv, m_send, m_recv, p_send, p_recv, d_send, d_recv, w_send, w_recv, b_send, b_recv,
):
    at = (lax.axis_index(X), lax.axis_index(Y), lax.axis_index(Z))
    x, y, z = at
    c = lax.axis_index(C)
    names = (X, Y, Z)

    def near(axis, step):
        return lax.rem(at[axis] + step, 4)

    barrier = pltpu.get_barrier_semaphore()
    pl.semaphore_signal(barrier, inc=1, device_id={C: 1 - c}, device_id_type=MESH_ID)
    for axis in range(3):
        for step in (1, 2, 3):
            pl.semaphore_signal(
                barrier, inc=1, device_id={names[axis]: near(axis, step)}, device_id_type=MESH_ID
            )
    loads = [
        pltpu.make_async_copy(src, dst, load_sem.at[n])
        for n, (src, dst) in enumerate(
            ((w_in, wbuf), (k_hbm, k), (v_hbm, v), (q_hbm, q), (g_hbm, g))
        )
    ]
    for load in loads:
        load.start()

    place = z * 2 + c
    own_id = [ids[place * 4 + b] for b in range(4)]
    row = lax.broadcasted_iota(jnp.int32, (BLK, BLK), 0)
    column = lax.broadcasted_iota(jnp.int32, (BLK, BLK), 1)
    for b in range(4):
        part = slice(b * BLK, b * BLK + BLK)
        keep_n[part, :] = (SBLK - 1.0 - b * BLK) - row.astype(F32) + same(own_id[b], own_id[3], 0.0)
        last = jnp.where(own_id[b] == own_id[3], 1.0, 0.0)
        lasting[part, :] = jnp.full((BLK, DH), last, F32).astype(BF16)

    def cols(h):
        return pl.ds(pl.multiple_of(h * DH, DH), DH)

    def states(into, first):
        @pl.loop(0, 8)
        def _(i):
            h = first + i
            values = v[:, cols(h)]
            lost = lasting[...].astype(F32) - jnp.exp(-rates[h] * keep_n[...])
            pair = jnp.concatenate([values * lasting[...], values * lost.astype(BF16)], axis=1)
            both = dot(k[:, cols(h)], pair, 0, 0)
            into[i] = both[:, :DH] - both[:, DH:]

    def attend(low, high):
        @pl.loop(low, high)
        def _(h):
            rate = rates[h]
            queries, keys, values = q[:, cols(h)], k[:, cols(h)], v[:, cols(h)]
            ahead = row - column
            base = jnp.exp(-rate * ahead.astype(F32))

            def weigh(scores, bi, bj):
                if bj > bi:
                    return jnp.zeros((BLK, BLK), BF16)
                table = jnp.where(ahead >= 0, base, 0.0) if bi == bj else base
                n = same(own_id[bi], own_id[bj], float(BLK * (bi - bj)))
                return (scores * (table * decay(rate, n))).astype(BF16)

            for low_block in (0, 2):
                first = low_block * BLK
                scores = dot(queries[first:], keys[first : first + 256], 1, 1)
                weights = jnp.concatenate(
                    [
                        jnp.concatenate(
                            [
                                weigh(
                                    scores[bi * BLK - first : bi * BLK - first + BLK, j * BLK : j * BLK + BLK],
                                    bi, low_block + j,
                                )
                                for j in range(2)
                            ],
                            axis=1,
                        )
                        for bi in range(low_block, 4)
                    ],
                    axis=0,
                )
                part = dot(weights, values[first : first + 256], 1, 0)
                if low_block == 0:
                    total = part
            inner[h, :256, :] = total[:256]
            inner[h, 256:, :] = total[256:] + part
            gate = g[:, cols(h)].astype(F32)
            gated[h] = gain[:, cols(h)] * (gate / (1.0 + jnp.exp(-gate)))

    def remote(src, dst, send, recv, to):
        return pltpu.make_async_remote_copy(
            src_ref=src, dst_ref=dst, send_sem=send, recv_sem=recv, device_id=to, device_id_type=MESH_ID
        )

    SLOTS = ((1, 0), (1, 1), (3, 1), (3, 0), (1, 0), (3, 1))

    def phase_of(group):
        return min(group, 2)

    def piece(colour, group, coord, half):
        low, wide, order = COLOURS[colour]
        phase = phase_of(group)
        index = list(at) + [c]
        lanes = slice(low, low + wide)
        index[order[0]] = slice(0, 4) if half is None else slice(2 * half, 2 * half + 2)
        if phase == 2:
            index[order[1]] = near(order[1], group - 2)
        index[order[phase]] = coord
        return tuple(index) + (slice(None), lanes)

    started = []

    def ring_copy(colour, group, slot, step, coord, half):
        axis = COLOURS[colour][2][phase_of(group)]
        where = piece(colour, group, coord, half)
        return remote(
            w_all.at[where], w_all.at[where], w_send.at[colour, group, slot], w_recv.at[colour, group, slot],
            {names[axis]: near(axis, step)},
        )

    def direct_copy(colour, step, coord):
        low, wide, order = COLOURS[colour]
        index = list(at) + [c]
        index[order[0]] = coord
        return remote(
            wbuf.at[:, low : low + wide], w_all.at[tuple(index) + (slice(None), slice(low, low + wide))],
            w_send.at[colour, 0, step], w_recv.at[colour, 0, step], {names[order[0]]: near(order[0], step)},
        )

    def line_start():
        for colour in range(3):
            for step in (1, 3, 2):
                copy = direct_copy(colour, step, at[COLOURS[colour][2][0]])
                copy.start()
                started.append(copy)

    def line_end():
        for colour in range(3):
            axis = COLOURS[colour][2][0]
            for step in (1, 3, 2):
                direct_copy(colour, step, near(axis, 4 - step)).wait_recv()
        for colour in range(3):
            twin(piece(colour, 1, at[COLOURS[colour][2][1]], None), 18 * colour)

    def ring_start(group):
        for colour in range(3):
            mine = at[COLOURS[colour][2][phase_of(group)]]
            for slot in (0, 2, 1, 3):
                step, half = SLOTS[slot]
                copy = ring_copy(colour, group, slot, step, mine, half)
                copy.start()
                started.append(copy)

    def ring_pass(group):
        for colour in range(3):
            axis = COLOURS[colour][2][phase_of(group)]
            for slot in (0, 2):
                step, half = SLOTS[slot]
                from_coord = near(axis, 4 - step)
                ring_copy(colour, group, slot, step, from_coord, half).wait_recv()
                copy = ring_copy(colour, group, 4 if slot == 0 else 5, step, from_coord, half)
                copy.start()
                started.append(copy)

    twins = []

    def twin(where, slot):
        copy = remote(w_all.at[where], w_all.at[where], b_send.at[slot], b_recv.at[slot], {C: 1 - c})
        copy.start()
        started.append(copy)
        twins.append((where[:3] + (1 - c,) + where[4:], slot))

    def ring_end(group):
        for colour in range(3):
            axis = COLOURS[colour][2][phase_of(group)]
            for slot in (1, 3):
                step, half = SLOTS[slot]
                ring_copy(colour, group, slot, step, near(axis, 4 - step), half).wait_recv()
            twin(piece(colour, group, near(axis, 1), None), 18 * colour + 3 * group)
            twin(piece(colour, group, near(axis, 3), None), 18 * colour + 3 * group + 1)
        for colour in range(3):
            axis = COLOURS[colour][2][phase_of(group)]
            for slot in (4, 5):
                step, half = SLOTS[slot]
                ring_copy(colour, group, slot, step, near(axis, 2), half).wait_recv()
            twin(piece(colour, group, near(axis, 2), None), 18 * colour + 3 * group + 2)

    def twin_waits():
        for where, slot in twins:
            view = w_all.at[where]
            remote(view, view, b_send.at[slot], b_recv.at[slot], {C: 1 - c}).wait_recv()

    pl.semaphore_wait(barrier, 10)
    loads[0].wait()
    line_start()
    own_store = pltpu.make_async_copy(wbuf, w_all.at[x, y, z, c], store_sem.at[2])
    own_store.start()
    loads[1].wait()
    loads[2].wait()
    states(s_out, (1 - c) * 8)
    core_copy = remote(s_out, s_in, c_send, c_recv, {C: 1 - c})
    core_copy.start()
    states(s_own, c * 8)
    core_copy.wait()

    chip = z * 8
    n_first = jnp.where(c == 0, same(ids[chip + 3], ids[chip + 7], 512.0), 0.0)
    n_second = jnp.where(c == 1, same(ids[chip + 3], ids[chip + 7], 512.0), 0.0)
    for i in range(8):
        rate = rates[c * 8 + i]
        both = s_own[i] * decay(rate, n_first) + s_in[i] * decay(rate, n_second)
        z_out[i // 2, (i % 2) * DH : (i % 2) * DH + DH, :] = both.astype(BF16)

    def spread(copies):
        for copy in copies:
            copy.start()
        return copies

    def settle(copies):
        for copy in copies:
            copy.wait()

    line_copies = spread([
        remote(
            z_out.at[near(2, step)], z_in.at[3 - step], z_send.at[step - 1], z_recv.at[3 - step],
            {Z: near(2, step)},
        )
        for step in (1, 3, 2)
    ])
    loads[3].wait()
    loads[4].wait()
    own_store.wait()
    line_end()
    ring_start(1)
    attend(0, 2)
    ring_pass(1)
    ring_start(2)
    attend(2, 5)
    settle(line_copies)

    two = [rates[c * 8 + z * 2 + j] for j in range(2)]
    spots = [near(2, step) for step in range(4)]
    line_first, line_last = ids[0], ids[31]
    halves = (slice(0, DH), slice(DH, 2 * DH))

    def held(step, j):
        block = z_out[z, halves[j], :] if step == 0 else z_in[step - 1, halves[j], :]
        return block.astype(F32)

    for j, out in enumerate((y_out, x_out)):
        total = None
        for step in range(4):
            spot = spots[step]
            n = same(ids[spot * 8 + 7], line_last, (1024 * (3 - spot)).astype(F32))
            term = held(step, j) * decay(two[j], n)
            total = term if total is None else total + term
        out[:DH, :] = total.astype(BF16)
        note_row = lax.broadcasted_iota(jnp.int32, (16, DH), 0)
        notes = jnp.where(note_row < 8, line_last.astype(F32), line_first.astype(F32))
        out[DH : DH + 16, :] = notes.astype(BF16)
    column_copies = spread(
        [
            remote(
                src, into.at[3 - step], send.at[step - 1], recv.at[3 - step],
                {names[axis]: near(axis, step)},
            )
            for step in (1, 3, 2)
            for axis, src, into, send, recv in (
                (1, y_out, y_in, y_send, y_recv), (0, x_out, x_in, x_send, x_recv),
            )
        ]
    )
    for t in range(4):
        target = spots[t]
        for j in range(2):
            total = None
            for step in range(4):
                if step == t:
                    continue
                spot = spots[step]
                n = same(ids[spot * 8 + 7], ids[target * 8], (1024 * (target - 1 - spot)).astype(F32))
                term = held(step, j) * decay(two[j], jnp.where(spot < target, n, FAR))
                total = term if total is None else total + term
            p_part[t, halves[j], :] = total
    ring_end(1)
    ring_start(3)
    ring_pass(2)
    attend(5, 8)
    settle(column_copies)

    spots_y = [near(1, step) for step in range(4)]
    spots_x = [near(0, step) for step in range(4)]

    def view(own, came, step):
        return own if step == 0 else came.at[step - 1]

    def body_of(ref):
        return ref[:DH, :].astype(F32)

    def last_of(ref):
        return ref[DH : DH + 1, :].astype(F32)

    def first_of(ref):
        return ref[DH + 8 : DH + 9, :].astype(F32)

    by_y = [view(y_out, y_in, step) for step in range(4)]
    by_x = [view(x_out, x_in, step) for step in range(4)]
    slab_last = jnp.zeros((1, DH), F32)
    for step in range(4):
        slab_last = slab_last + jnp.where(spots_y[step] == 3, 1.0, 0.0) * last_of(by_y[step])
    total = None
    for step in range(4):
        spot = spots_y[step]
        n = same(last_of(by_y[step]), slab_last, (4096 * (3 - spot)).astype(F32))
        term = body_of(by_y[step]) * decay(two[0], n)
        total = term if total is None else total + term
    u_out[:DH, :] = total.astype(BF16)
    u_out[DH : DH + 16, :] = jnp.broadcast_to(slab_last, (16, DH)).astype(BF16)
    for t in range(4):
        target, first = spots_y[t], first_of(by_y[t])
        total = None
        for step in range(4):
            ref = by_x[step]
            if step == 0:
                n = same(last_of(ref), first, (4096 * (target - 1 - y)).astype(F32))
                n = jnp.where(y < target, n, FAR)
            else:
                spot = spots_x[step]
                lines = 4 * (x - spot) - y - 1 + target
                n = same(last_of(ref), first, (4096 * lines).astype(F32))
                n = jnp.where(spot < x, n, FAR)
            term = body_of(ref) * decay(two[1], n)
            total = term if total is None else total + term
        m_out[t] = total.astype(BF16)
    slab_copies = spread(
        [
            copy
            for step in (1, 3, 2)
            for copy in (
                remote(
                    u_out, u_in.at[3 - step], u_send.at[step - 1], u_recv.at[3 - step],
                    {X: near(0, step)},
                ),
                remote(
                    m_out.at[step], m_in.at[3 - step], m_send.at[step - 1], m_recv.at[3 - step],
                    {Y: near(1, step)},
                ),
            )
        ]
    )
    ring_end(2)
    ring_start(5)
    ring_pass(3)
    attend(8, 11)
    settle(slab_copies)

    total = jnp.zeros((DH, DH), F32)
    first = line_first.astype(F32)
    for step in range(1, 4):
        ref, spot = by_y[step], spots_y[step]
        n = same(last_of(ref), first, (4096 * (y - 1 - spot)).astype(F32))
        total = total + body_of(ref) * decay(two[0], jnp.where(spot < y, n, FAR))
        ref, spot = u_in.at[step - 1], spots_x[step]
        n = same(last_of(ref), first, (16384 * (x - 1 - spot) + 4096 * y).astype(F32))
        total = total + body_of(ref) * decay(two[0], jnp.where(spot < x, n, FAR))
    fronts = [total]
    total = m_out[0].astype(F32)
    for step in range(3):
        total = total + m_in[step].astype(F32)
    fronts.append(total)
    for t in range(4):
        n = same(line_first, ids[spots[t] * 8], (1024 * spots[t]).astype(F32))
        for j in range(2):
            whole = p_part[t, halves[j], :] + fronts[j] * decay(two[j], n)
            p_out[t, halves[j], :] = whole.astype(BF16)
    back_copies = spread([
        remote(
            p_out.at[step], p_in.at[3 - step], p_send.at[step - 1], p_recv.at[3 - step],
            {Z: near(2, step)},
        )
        for step in (1, 3, 2)
    ])
    ring_end(3)
    ring_start(4)
    ring_pass(5)
    attend(11, 16)
    settle(back_copies)

    n_chip = same(ids[chip], ids[chip + 4], 512.0)
    n_core = same(ids[chip + 3], ids[chip + 4], 0.0)
    mine = jnp.where(c == 1, n_core, FAR)
    theirs = jnp.where(c == 0, n_core, FAR)
    for step in range(4):
        for j in range(2):
            i = spots[step] * 2 + j
            rate = rates[c * 8 + i]
            before = (p_out[0, halves[j], :] if step == 0 else p_in[step - 1, halves[j], :]).astype(F32)
            own = before * decay(rate, jnp.where(c == 1, n_chip, 0.0)) + s_in[i] * decay(rate, mine)
            away = before * decay(rate, jnp.where(c == 0, n_chip, 0.0)) + s_own[i] * decay(rate, theirs)
            p_own[i] = own.astype(BF16)
            c_out[i] = away.astype(BF16)
    pair_copy = remote(c_out, c_in, d_send, d_recv, {C: 1 - c})
    pair_copy.start()
    ring_pass(4)

    def finish(first, ref):
        @pl.loop(0, 8)
        def _(i):
            h = first + i
            carried = dot(q[:, cols(h)], ref[i], 1, 0)
            base = jnp.exp(-rates[h] * (row.astype(F32) + 1.0))
            for b in range(4):
                part = slice(b * BLK, b * BLK + BLK)
                reach = base * decay(rates[h], same(own_id[b], own_id[0], float(b * BLK)))
                mixed = (inner[h, part, :] + carried[part] * reach).astype(BF16).astype(F32)
                inv = lax.rsqrt(jnp.mean(mixed * mixed, axis=-1, keepdims=True) + 1e-06)
                nrm[part, cols(h)] = (mixed * inv * gated[h, part, :]).astype(BF16)

    def put(first, slot):
        half = pl.ds(pl.multiple_of(first * DH, 1024), 1024)
        return pltpu.make_async_copy(nrm.at[:, half], nrm_hbm.at[:, half], store_sem.at[slot])

    finish(c * 8, p_own)
    put(c * 8, 0).start()
    ring_end(5)
    ring_end(4)
    pair_copy.wait()
    finish((1 - c) * 8, c_in)
    put((1 - c) * 8, 1).start()
    twin_waits()
    for copy in started:
        copy.wait_send()
    put(c * 8, 0).wait()
    put((1 - c) * 8, 1).wait()


def gather_and_attend(ids, rates, q, k, v, g, gain, w):
    tokens, width = q.shape
    heads = rates.shape[0]
    hbm = pl.BlockSpec(memory_space=pl.ANY)
    smem = pl.BlockSpec(memory_space=pltpu.SMEM)
    vmem = pltpu.VMEM
    dma = pltpu.SemaphoreType.DMA
    rows = w.shape[0]
    return pl.pallas_call(
        scan_kernel,
        out_shape=(
            jax.ShapeDtypeStruct((tokens, width), BF16),
            jax.ShapeDtypeStruct((4, 4, 4, 2, rows, width), BF16),
        ),
        in_specs=[smem, smem, hbm, hbm, hbm, hbm, pl.BlockSpec(memory_space=vmem), hbm],
        out_specs=(hbm, hbm),
        scratch_shapes=[
            vmem((tokens, width), BF16),
            vmem((tokens, width), BF16),
            vmem((tokens, width), BF16),
            vmem((tokens, width), BF16),
            vmem((rows, width), BF16),
            vmem((tokens, width), BF16),
            vmem((heads, tokens, DH), F32),
            vmem((heads, tokens, DH), F32),
            vmem((512, DH), F32),
            vmem((512, DH), BF16),
            vmem((8, DH, DH), F32),
            vmem((8, DH, DH), F32),
            vmem((8, DH, DH), F32),
            vmem((4, 2 * DH, DH), BF16),
            vmem((3, 2 * DH, DH), BF16),
            vmem((4, 2 * DH, DH), F32),
            vmem((DH + 16, DH), BF16),
            vmem((3, DH + 16, DH), BF16),
            vmem((DH + 16, DH), BF16),
            vmem((3, DH + 16, DH), BF16),
            vmem((DH + 16, DH), BF16),
            vmem((3, DH + 16, DH), BF16),
            vmem((4, DH, DH), BF16),
            vmem((3, DH, DH), BF16),
            vmem((4, 2 * DH, DH), BF16),
            vmem((3, 2 * DH, DH), BF16),
            vmem((8, DH, DH), BF16),
            vmem((8, DH, DH), BF16),
            vmem((8, DH, DH), BF16),
            dma((5,)),
            dma((3,)),
            dma, dma,
            dma((3,)), dma((3,)),
            dma((3,)), dma((3,)),
            dma((3,)), dma((3,)),
            dma((3,)), dma((3,)),
            dma((3,)), dma((3,)),
            dma((3,)), dma((3,)),
            dma, dma,
            dma((3, 6, 6)), dma((3, 6, 6)),
            dma((54,)), dma((54,)),
        ],
        compiler_params=pltpu.CompilerParams(
            collective_id=0, has_side_effects=True, vmem_limit_bytes=60 << 20
        ),
        name="scan_and_gather",
    )(ids, rates, q, k, v, g, gain, w)


def project_kernel(a, b, o):
    o[...] = jnp.dot(a[...], b[...], preferred_element_type=F32).astype(BF16)


def project(a, b):
    rows, depth = a.shape
    columns = b.shape[1]
    tile = 1024
    return pl.pallas_call(
        project_kernel,
        out_shape=jax.ShapeDtypeStruct((rows, columns), BF16),
        grid=(columns // tile,),
        in_specs=[
            pl.BlockSpec((rows, depth), lambda j: (0, 0)),
            pl.BlockSpec((depth, tile), lambda j: (0, j)),
        ],
        out_specs=pl.BlockSpec((rows, tile), lambda j: (0, j)),
        compiler_params=pltpu.CompilerParams(vmem_limit_bytes=60 << 20),
        name="project",
    )(a, b)


def on_device(query_rows, key_rows, value_rows, gate_rows, segment_ids, decay_rates, norm_gain, out_weight):
    width = query_rows.shape[1]
    normed, weight = gather_and_attend(
        segment_ids, decay_rates, query_rows, key_rows, value_rows, gate_rows,
        norm_gain.reshape(1, width), out_weight,
    )
    return project(normed, weight.reshape(width, width))


def solution(mesh):
    split = Mesh(mesh.devices.reshape(4, 4, 4, 2), SEQ_HEAD)
    rows = P(SEQ_HEAD, None)
    return jax.shard_map(
        on_device,
        mesh=split,
        in_specs=(rows, rows, rows, rows, P(SEQ), P(), P(), rows),
        out_specs=rows,
        check_vma=False,
    )
```

```python
import functools

import jax
import jax.numpy as jnp
from jax import lax
from jax.experimental import pallas as pl
from jax.experimental.pallas import tpu as pltpu
from jax.sharding import Mesh
from jax.sharding import PartitionSpec as P

BLK = 128
SBLK = 512
DH = 128
FAR = 1e30
X, Y, Z, C = "seq_0", "seq_1", "head_0", "head_1"
SEQ_HEAD = (X, Y, Z, C)
SEQ = (X, Y)
MESH_ID = pl.DeviceIdType.MESH
F32, BF16 = jnp.float32, jnp.bfloat16

COLOURS = (
    (0, 768, (2, 1, 0)),
    (768, 512, (1, 0, 2)),
    (1280, 768, (0, 2, 1)),
)


def dot(a, b, ca, cb):
    return lax.dot_general(a, b, (((ca,), (cb,)), ((), ())), preferred_element_type=F32)


def same(a, b, n):
    return jnp.where(a == b, n, FAR)


def decay(rate, n):
    return jnp.exp(-rate * jnp.broadcast_to(n, (1, DH)))


def scan_kernel(
    ids, rates, q_hbm, k_hbm, v_hbm, g_hbm, gain, w_in,
    out_hbm,
    q, k, v, g, w_all, nrm, mixed_out, inner, gated, keep_n, lasting,
    s_own, s_out, s_in, z_out, z_in, p_part, y_out, y_in, x_out, x_in, u_out, u_in, m_out, m_in,
    p_out, p_in, c_out, c_in, p_own,
    load_sem, store_sem, c_send, c_recv, z_send, z_recv, y_send, y_recv, x_send, x_recv,
    u_send, u_recv, m_send, m_recv, p_send, p_recv, d_send, d_recv, w_send, w_recv, b_send, b_recv,
):
    at = (lax.axis_index(X), lax.axis_index(Y), lax.axis_index(Z))
    x, y, z = at
    c = lax.axis_index(C)
    names = (X, Y, Z)

    def near(axis, step):
        return lax.rem(at[axis] + step, 4)

    barrier = pltpu.get_barrier_semaphore()
    pl.semaphore_signal(barrier, inc=1, device_id={C: 1 - c}, device_id_type=MESH_ID)
    for axis in range(3):
        for step in (1, 2, 3):
            pl.semaphore_signal(
                barrier, inc=1, device_id={names[axis]: near(axis, step)}, device_id_type=MESH_ID
            )
    loads = [
        pltpu.make_async_copy(src, dst, load_sem.at[n])
        for n, (src, dst) in enumerate(
            ((w_in, w_all.at[x, y, z, c]), (k_hbm, k), (v_hbm, v), (q_hbm, q), (g_hbm, g))
        )
    ]
    for load in loads:
        load.start()

    place = z * 2 + c
    own_id = [ids[place * 4 + b] for b in range(4)]
    row = lax.broadcasted_iota(jnp.int32, (BLK, BLK), 0)
    column = lax.broadcasted_iota(jnp.int32, (BLK, BLK), 1)
    for b in range(4):
        part = slice(b * BLK, b * BLK + BLK)
        keep_n[part, :] = (SBLK - 1.0 - b * BLK) - row.astype(F32) + same(own_id[b], own_id[3], 0.0)
        last = jnp.where(own_id[b] == own_id[3], 1.0, 0.0)
        lasting[part, :] = jnp.full((BLK, DH), last, F32).astype(BF16)

    def cols(h):
        return pl.ds(pl.multiple_of(h * DH, DH), DH)

    def states(into, first):
        @pl.loop(0, 8, unroll=4)
        def _(i):
            h = first + i
            values = v[:, cols(h)]
            lost = lasting[...].astype(F32) - jnp.exp(-rates[h] * keep_n[...])
            pair = jnp.concatenate([values * lasting[...], values * lost.astype(BF16)], axis=1)
            both = dot(k[:, cols(h)], pair, 0, 0)
            into[i] = both[:, :DH] - both[:, DH:]

    def attend(low, high):
        @pl.loop(low, high)
        def _(h):
            rate = rates[h]
            queries, keys, values = q[:, cols(h)], k[:, cols(h)], v[:, cols(h)]
            ahead = row - column
            base = jnp.exp(-rate * ahead.astype(F32))

            def weigh(scores, bi, bj):
                if bj > bi:
                    return jnp.zeros((BLK, BLK), BF16)
                table = jnp.where(ahead >= 0, base, 0.0) if bi == bj else base
                n = same(own_id[bi], own_id[bj], float(BLK * (bi - bj)))
                return (scores * (table * decay(rate, n))).astype(BF16)

            for low_block in (0, 2):
                first = low_block * BLK
                scores = dot(queries[first:], keys[first : first + 256], 1, 1)
                weights = jnp.concatenate(
                    [
                        jnp.concatenate(
                            [
                                weigh(
                                    scores[bi * BLK - first : bi * BLK - first + BLK, j * BLK : j * BLK + BLK],
                                    bi, low_block + j,
                                )
                                for j in range(2)
                            ],
                            axis=1,
                        )
                        for bi in range(low_block, 4)
                    ],
                    axis=0,
                )
                part = dot(weights, values[first : first + 256], 1, 0)
                if low_block == 0:
                    total = part
            inner[h, :256, :] = total[:256]
            inner[h, 256:, :] = total[256:] + part
            gate = g[:, cols(h)].astype(F32)
            gated[h] = gain[:, cols(h)] * (gate / (1.0 + jnp.exp(-gate)))

    def remote(src, dst, send, recv, to):
        return pltpu.make_async_remote_copy(
            src_ref=src, dst_ref=dst, send_sem=send, recv_sem=recv, device_id=to, device_id_type=MESH_ID
        )

    SLOTS = ((1, 0), (1, 1), (3, 1), (3, 0), (1, 0), (3, 1))

    def phase_of(group):
        return min(group, 2)

    def piece(colour, group, coord, half):
        low, wide, order = COLOURS[colour]
        phase = phase_of(group)
        index = list(at) + [c]
        lanes = slice(low, low + wide)
        index[order[0]] = slice(0, 4) if half is None else slice(2 * half, 2 * half + 2)
        if phase == 2:
            index[order[1]] = near(order[1], group - 2)
        index[order[phase]] = coord
        return tuple(index) + (slice(None), lanes)

    started = []

    def ring_copy(colour, group, slot, step, coord, half):
        axis = COLOURS[colour][2][phase_of(group)]
        where = piece(colour, group, coord, half)
        return remote(
            w_all.at[where], w_all.at[where], w_send.at[colour, group, slot], w_recv.at[colour, group, slot],
            {names[axis]: near(axis, step)},
        )

    def direct_copy(colour, step, coord):
        low, wide, order = COLOURS[colour]
        index = list(at) + [c]
        index[order[0]] = coord
        return remote(
            w_all.at[x, y, z, c, :, low : low + wide],
            w_all.at[tuple(index) + (slice(None), slice(low, low + wide))],
            w_send.at[colour, 0, step], w_recv.at[colour, 0, step], {names[order[0]]: near(order[0], step)},
        )

    def line_start():
        for colour in range(3):
            for step in (1, 3, 2):
                copy = direct_copy(colour, step, at[COLOURS[colour][2][0]])
                copy.start()
                started.append(copy)

    def line_end():
        for colour in range(3):
            axis = COLOURS[colour][2][0]
            for step in (1, 3, 2):
                direct_copy(colour, step, near(axis, 4 - step)).wait_recv()
        for colour in range(3):
            twin(piece(colour, 1, at[COLOURS[colour][2][1]], None), 18 * colour)

    def ring_start(group):
        for colour in range(3):
            mine = at[COLOURS[colour][2][phase_of(group)]]
            for slot in (0, 2, 1, 3):
                step, half = SLOTS[slot]
                copy = ring_copy(colour, group, slot, step, mine, half)
                copy.start()
                started.append(copy)

    def ring_pass(group):
        for colour in range(3):
            axis = COLOURS[colour][2][phase_of(group)]
            for slot in (0, 2):
                step, half = SLOTS[slot]
                from_coord = near(axis, 4 - step)
                ring_copy(colour, group, slot, step, from_coord, half).wait_recv()
                copy = ring_copy(colour, group, 4 if slot == 0 else 5, step, from_coord, half)
                copy.start()
                started.append(copy)

    twins = []

    def twin(where, slot):
        copy = remote(w_all.at[where], w_all.at[where], b_send.at[slot], b_recv.at[slot], {C: 1 - c})
        copy.start()
        started.append(copy)
        twins.append((where[:3] + (1 - c,) + where[4:], slot))

    def ring_near(group):
        for colour in range(3):
            axis = COLOURS[colour][2][phase_of(group)]
            for slot in (1, 3):
                step, half = SLOTS[slot]
                ring_copy(colour, group, slot, step, near(axis, 4 - step), half).wait_recv()
            twin(piece(colour, group, near(axis, 1), None), 18 * colour + 3 * group)
            twin(piece(colour, group, near(axis, 3), None), 18 * colour + 3 * group + 1)

    def ring_far(group):
        for colour in range(3):
            axis = COLOURS[colour][2][phase_of(group)]
            for slot in (4, 5):
                step, half = SLOTS[slot]
                ring_copy(colour, group, slot, step, near(axis, 2), half).wait_recv()
            twin(piece(colour, group, near(axis, 2), None), 18 * colour + 3 * group + 2)

    def twin_waits():
        for where, slot in twins:
            view = w_all.at[where]
            remote(view, view, b_send.at[slot], b_recv.at[slot], {C: 1 - c}).wait_recv()

    pl.semaphore_wait(barrier, 10)
    loads[0].wait()
    line_start()
    loads[1].wait()
    loads[2].wait()
    states(s_out, (1 - c) * 8)
    core_copy = remote(s_out, s_in, c_send, c_recv, {C: 1 - c})
    core_copy.start()
    line_end()
    ring_start(1)
    states(s_own, c * 8)
    core_copy.wait()

    chip = z * 8
    n_first = jnp.where(c == 0, same(ids[chip + 3], ids[chip + 7], 512.0), 0.0)
    n_second = jnp.where(c == 1, same(ids[chip + 3], ids[chip + 7], 512.0), 0.0)
    for i in range(8):
        rate = rates[c * 8 + i]
        both = s_own[i] * decay(rate, n_first) + s_in[i] * decay(rate, n_second)
        z_out[i // 2, (i % 2) * DH : (i % 2) * DH + DH, :] = both.astype(BF16)

    def spread(copies):
        for copy in copies:
            copy.start()
        return copies

    def settle(copies):
        for copy in copies:
            copy.wait()

    line_copies = spread([
        remote(
            z_out.at[near(2, step)], z_in.at[3 - step], z_send.at[step - 1], z_recv.at[3 - step],
            {Z: near(2, step)},
        )
        for step in (1, 3, 2)
    ])
    loads[3].wait()
    loads[4].wait()
    ring_pass(1)
    ring_near(1)
    ring_start(3)
    attend(0, 3)
    ring_start(5)
    attend(3, 5)
    settle(line_copies)

    two = [rates[c * 8 + z * 2 + j] for j in range(2)]
    spots = [near(2, step) for step in range(4)]
    line_first, line_last = ids[0], ids[31]
    halves = (slice(0, DH), slice(DH, 2 * DH))

    def held(step, j):
        block = z_out[z, halves[j], :] if step == 0 else z_in[step - 1, halves[j], :]
        return block.astype(F32)

    for j, out in enumerate((y_out, x_out)):
        total = None
        for step in range(4):
            spot = spots[step]
            n = same(ids[spot * 8 + 7], line_last, (1024 * (3 - spot)).astype(F32))
            term = held(step, j) * decay(two[j], n)
            total = term if total is None else total + term
        out[:DH, :] = total.astype(BF16)
        note_row = lax.broadcasted_iota(jnp.int32, (16, DH), 0)
        notes = jnp.where(note_row < 8, line_last.astype(F32), line_first.astype(F32))
        out[DH : DH + 16, :] = notes.astype(BF16)
    column_copies = spread(
        [
            remote(
                src, into.at[3 - step], send.at[step - 1], recv.at[3 - step],
                {names[axis]: near(axis, step)},
            )
            for step in (1, 3, 2)
            for axis, src, into, send, recv in (
                (1, y_out, y_in, y_send, y_recv), (0, x_out, x_in, x_send, x_recv),
            )
        ]
    )
    for t in range(4):
        target = spots[t]
        for j in range(2):
            total = None
            for step in range(4):
                if step == t:
                    continue
                spot = spots[step]
                n = same(ids[spot * 8 + 7], ids[target * 8], (1024 * (target - 1 - spot)).astype(F32))
                term = held(step, j) * decay(two[j], jnp.where(spot < target, n, FAR))
                total = term if total is None else total + term
            p_part[t, halves[j], :] = total
    ring_pass(3)
    ring_far(1)
    ring_start(4)
    attend(5, 8)
    settle(column_copies)

    spots_y = [near(1, step) for step in range(4)]
    spots_x = [near(0, step) for step in range(4)]

    def view(own, came, step):
        return own if step == 0 else came.at[step - 1]

    def body_of(ref):
        return ref[:DH, :].astype(F32)

    def last_of(ref):
        return ref[DH : DH + 1, :].astype(F32)

    def first_of(ref):
        return ref[DH + 8 : DH + 9, :].astype(F32)

    by_y = [view(y_out, y_in, step) for step in range(4)]
    by_x = [view(x_out, x_in, step) for step in range(4)]
    slab_last = jnp.zeros((1, DH), F32)
    for step in range(4):
        slab_last = slab_last + jnp.where(spots_y[step] == 3, 1.0, 0.0) * last_of(by_y[step])
    total = None
    for step in range(4):
        spot = spots_y[step]
        n = same(last_of(by_y[step]), slab_last, (4096 * (3 - spot)).astype(F32))
        term = body_of(by_y[step]) * decay(two[0], n)
        total = term if total is None else total + term
    u_out[:DH, :] = total.astype(BF16)
    u_out[DH : DH + 16, :] = jnp.broadcast_to(slab_last, (16, DH)).astype(BF16)
    for t in range(4):
        target, first = spots_y[t], first_of(by_y[t])
        total = None
        for step in range(4):
            ref = by_x[step]
            if step == 0:
                n = same(last_of(ref), first, (4096 * (target - 1 - y)).astype(F32))
                n = jnp.where(y < target, n, FAR)
            else:
                spot = spots_x[step]
                lines = 4 * (x - spot) - y - 1 + target
                n = same(last_of(ref), first, (4096 * lines).astype(F32))
                n = jnp.where(spot < x, n, FAR)
            term = body_of(ref) * decay(two[1], n)
            total = term if total is None else total + term
        m_out[t] = total.astype(BF16)
    slab_copies = spread(
        [
            copy
            for step in (1, 3, 2)
            for copy in (
                remote(
                    u_out, u_in.at[3 - step], u_send.at[step - 1], u_recv.at[3 - step],
                    {X: near(0, step)},
                ),
                remote(
                    m_out.at[step], m_in.at[3 - step], m_send.at[step - 1], m_recv.at[3 - step],
                    {Y: near(1, step)},
                ),
            )
        ]
    )
    ring_pass(5)
    ring_start(2)
    attend(8, 9)
    ring_pass(4)
    attend(9, 11)
    settle(slab_copies)

    total = jnp.zeros((DH, DH), F32)
    first = line_first.astype(F32)
    for step in range(1, 4):
        ref, spot = by_y[step], spots_y[step]
        n = same(last_of(ref), first, (4096 * (y - 1 - spot)).astype(F32))
        total = total + body_of(ref) * decay(two[0], jnp.where(spot < y, n, FAR))
        ref, spot = u_in.at[step - 1], spots_x[step]
        n = same(last_of(ref), first, (16384 * (x - 1 - spot) + 4096 * y).astype(F32))
        total = total + body_of(ref) * decay(two[0], jnp.where(spot < x, n, FAR))
    fronts = [total]
    total = m_out[0].astype(F32)
    for step in range(3):
        total = total + m_in[step].astype(F32)
    fronts.append(total)
    for t in range(4):
        n = same(line_first, ids[spots[t] * 8], (1024 * spots[t]).astype(F32))
        for j in range(2):
            whole = p_part[t, halves[j], :] + fronts[j] * decay(two[j], n)
            p_out[t, halves[j], :] = whole.astype(BF16)
    back_copies = spread([
        remote(
            p_out.at[step], p_in.at[3 - step], p_send.at[step - 1], p_recv.at[3 - step],
            {Z: near(2, step)},
        )
        for step in (1, 3, 2)
    ])
    ring_near(3)
    ring_far(3)
    ring_near(5)
    ring_far(5)
    attend(11, 12)
    ring_pass(2)
    attend(12, 14)
    ring_near(4)
    ring_far(4)
    attend(14, 16)
    settle(back_copies)

    n_chip = same(ids[chip], ids[chip + 4], 512.0)
    n_core = same(ids[chip + 3], ids[chip + 4], 0.0)
    mine = jnp.where(c == 1, n_core, FAR)
    theirs = jnp.where(c == 0, n_core, FAR)
    for step in range(4):
        for j in range(2):
            i = spots[step] * 2 + j
            rate = rates[c * 8 + i]
            before = (p_out[0, halves[j], :] if step == 0 else p_in[step - 1, halves[j], :]).astype(F32)
            own = before * decay(rate, jnp.where(c == 1, n_chip, 0.0)) + s_in[i] * decay(rate, mine)
            away = before * decay(rate, jnp.where(c == 0, n_chip, 0.0)) + s_own[i] * decay(rate, theirs)
            p_own[i] = own.astype(BF16)
            c_out[i] = away.astype(BF16)
    pair_copy = remote(c_out, c_in, d_send, d_recv, {C: 1 - c})
    pair_copy.start()
    ring_near(2)
    ring_far(2)

    def finish(first, ref):
        @pl.loop(0, 8, unroll=4)
        def _(i):
            h = first + i
            carried = dot(q[:, cols(h)], ref[i], 1, 0)
            base = jnp.exp(-rates[h] * (row.astype(F32) + 1.0))
            for b in range(4):
                part = slice(b * BLK, b * BLK + BLK)
                reach = base * decay(rates[h], same(own_id[b], own_id[0], float(b * BLK)))
                mixed = (inner[h, part, :] + carried[part] * reach).astype(BF16).astype(F32)
                inv = lax.rsqrt(jnp.mean(mixed * mixed, axis=-1, keepdims=True) + 1e-06)
                nrm[part, cols(h)] = (mixed * inv * gated[h, part, :]).astype(BF16)

    finish(c * 8, p_own)
    pair_copy.wait()
    finish((1 - c) * 8, c_in)
    twin_waits()

    def leave(n):
        lanes = pl.ds(pl.multiple_of(n * 512, 512), 512)
        return pltpu.make_async_copy(mixed_out.at[:, lanes], out_hbm.at[:, lanes], store_sem.at[n])

    @pl.loop(0, 4)
    def _(n):
        lanes = pl.ds(pl.multiple_of(n * 512, 512), 512)
        weight = w_all[:, :, :, :, :, lanes].reshape(2048, 512)
        mixed_out[:, lanes] = dot(nrm[...], weight, 1, 0).astype(BF16)
        leave(n).start()

    for copy in started:
        copy.wait_send()
    for n in range(4):
        leave(n).wait()


def gather_and_attend(ids, rates, q, k, v, g, gain, w):
    tokens, width = q.shape
    heads = rates.shape[0]
    hbm = pl.BlockSpec(memory_space=pl.ANY)
    smem = pl.BlockSpec(memory_space=pltpu.SMEM)
    vmem = pltpu.VMEM
    dma = pltpu.SemaphoreType.DMA
    rows = w.shape[0]
    return pl.pallas_call(
        scan_kernel,
        out_shape=jax.ShapeDtypeStruct((tokens, width), BF16),
        in_specs=[smem, smem, hbm, hbm, hbm, hbm, pl.BlockSpec(memory_space=vmem), hbm],
        out_specs=hbm,
        scratch_shapes=[
            vmem((tokens, width), BF16),
            vmem((tokens, width), BF16),
            vmem((tokens, width), BF16),
            vmem((tokens, width), BF16),
            vmem((4, 4, 4, 2, rows, width), BF16),
            vmem((tokens, width), BF16),
            vmem((tokens, width), BF16),
            vmem((heads, tokens, DH), F32),
            vmem((heads, tokens, DH), F32),
            vmem((512, DH), F32),
            vmem((512, DH), BF16),
            vmem((8, DH, DH), F32),
            vmem((8, DH, DH), F32),
            vmem((8, DH, DH), F32),
            vmem((4, 2 * DH, DH), BF16),
            vmem((3, 2 * DH, DH), BF16),
            vmem((4, 2 * DH, DH), F32),
            vmem((DH + 16, DH), BF16),
            vmem((3, DH + 16, DH), BF16),
            vmem((DH + 16, DH), BF16),
            vmem((3, DH + 16, DH), BF16),
            vmem((DH + 16, DH), BF16),
            vmem((3, DH + 16, DH), BF16),
            vmem((4, DH, DH), BF16),
            vmem((3, DH, DH), BF16),
            vmem((4, 2 * DH, DH), BF16),
            vmem((3, 2 * DH, DH), BF16),
            vmem((8, DH, DH), BF16),
            vmem((8, DH, DH), BF16),
            vmem((8, DH, DH), BF16),
            dma((5,)),
            dma((8,)),
            dma, dma,
            dma((3,)), dma((3,)),
            dma((3,)), dma((3,)),
            dma((3,)), dma((3,)),
            dma((3,)), dma((3,)),
            dma((3,)), dma((3,)),
            dma((3,)), dma((3,)),
            dma, dma,
            dma((3, 6, 6)), dma((3, 6, 6)),
            dma((54,)), dma((54,)),
        ],
        compiler_params=pltpu.CompilerParams(
            collective_id=0, has_side_effects=True, vmem_limit_bytes=60 << 20
        ),
        name="scan_and_gather",
    )(ids, rates, q, k, v, g, gain, w)


def on_device(query_rows, key_rows, value_rows, gate_rows, segment_ids, decay_rates, norm_gain, out_weight):
    width = query_rows.shape[1]
    return gather_and_attend(
        segment_ids, decay_rates, query_rows, key_rows, value_rows, gate_rows,
        norm_gain.reshape(1, width), out_weight,
    )


def solution(mesh):
    split = Mesh(mesh.devices.reshape(4, 4, 4, 2), SEQ_HEAD)
    rows = P(SEQ_HEAD, None)
    return jax.shard_map(
        on_device,
        mesh=split,
        in_specs=(rows, rows, rows, rows, P(SEQ), P(), P(), rows),
        out_specs=rows,
        check_vma=False,
    )
```

```python
import functools

import jax
import jax.numpy as jnp
from jax import lax
from jax.experimental import pallas as pl
from jax.experimental.pallas import tpu as pltpu
from jax.sharding import Mesh
from jax.sharding import PartitionSpec as P

BLK = 128
SBLK = 512
DH = 128
FAR = 1e30
X, Y, Z, C = "seq_0", "seq_1", "head_0", "head_1"
SEQ_HEAD = (X, Y, Z, C)
SEQ = (X, Y)
MESH_ID = pl.DeviceIdType.MESH
F32, BF16 = jnp.float32, jnp.bfloat16

COLOURS = (
    (0, 768, (2, 1, 0)),
    (768, 512, (1, 0, 2)),
    (1280, 768, (0, 2, 1)),
)


def dot(a, b, ca, cb):
    return lax.dot_general(a, b, (((ca,), (cb,)), ((), ())), preferred_element_type=F32)


def same(a, b, n):
    return jnp.where(a == b, n, FAR)


def decay(rate, n):
    return jnp.exp(-rate * jnp.broadcast_to(n, (1, DH)))


def scan_kernel(
    ids_hbm, rates_hbm, q_hbm, k_hbm, v_hbm, g_hbm, gain_hbm, w_in,
    mixed_out,
    ids, rates, gain, q, k, v, g, w_all, nrm, inner, gated, keep_n, lasting,
    s_own, s_out, s_in, z_out, z_in, p_part, y_out, y_in, x_out, x_in, u_out, u_in, m_out, m_in,
    p_out, p_in, c_out, c_in, p_own,
    load_sem, c_send, c_recv, z_send, z_recv, y_send, y_recv, x_send, x_recv,
    u_send, u_recv, m_send, m_recv, p_send, p_recv, d_send, d_recv, w_send, w_recv, b_send, b_recv,
):
    at = (lax.axis_index(X), lax.axis_index(Y), lax.axis_index(Z))
    x, y, z = at
    c = lax.axis_index(C)
    names = (X, Y, Z)

    def near(axis, step):
        return lax.rem(at[axis] + step, 4)

    barrier = pltpu.get_barrier_semaphore()
    pl.semaphore_signal(barrier, inc=1, device_id={C: 1 - c}, device_id_type=MESH_ID)
    for axis in range(3):
        for step in (1, 2, 3):
            pl.semaphore_signal(
                barrier, inc=1, device_id={names[axis]: near(axis, step)}, device_id_type=MESH_ID
            )
    loads = [
        pltpu.make_async_copy(src, dst, load_sem.at[n])
        for n, (src, dst) in enumerate(
            ((w_in, w_all.at[x, y, z, c]), (k_hbm, k), (v_hbm, v), (q_hbm, q), (g_hbm, g),
             (ids_hbm, ids), (rates_hbm, rates), (gain_hbm, gain))
        )
    ]
    for n in (5, 6, 0, 1, 2, 3, 4, 7):
        loads[n].start()
    loads[5].wait()
    loads[6].wait()

    place = z * 2 + c
    own_id = [ids[place * 4 + b] for b in range(4)]
    row = lax.broadcasted_iota(jnp.int32, (BLK, BLK), 0)
    column = lax.broadcasted_iota(jnp.int32, (BLK, BLK), 1)
    for b in range(4):
        part = slice(b * BLK, b * BLK + BLK)
        keep_n[part, :] = (SBLK - 1.0 - b * BLK) - row.astype(F32) + same(own_id[b], own_id[3], 0.0)
        last = jnp.where(own_id[b] == own_id[3], 1.0, 0.0)
        lasting[part, :] = jnp.full((BLK, DH), last, F32).astype(BF16)

    def cols(h):
        return pl.ds(pl.multiple_of(h * DH, DH), DH)

    def states(into, first):
        @pl.loop(0, 8, unroll=4)
        def _(i):
            h = first + i
            values = v[:, cols(h)]
            lost = lasting[...].astype(F32) - jnp.exp(-rates[h] * keep_n[...])
            pair = jnp.concatenate([values * lasting[...], values * lost.astype(BF16)], axis=1)
            both = dot(k[:, cols(h)], pair, 0, 0)
            into[i] = both[:, :DH] - both[:, DH:]

    def attend(low, high):
        @pl.loop(low, high)
        def _(h):
            rate = rates[h]
            queries, keys, values = q[:, cols(h)], k[:, cols(h)], v[:, cols(h)]
            ahead = row - column
            base = jnp.exp(-rate * ahead.astype(F32))

            def weigh(scores, bi, bj):
                if bj > bi:
                    return jnp.zeros((BLK, BLK), BF16)
                table = jnp.where(ahead >= 0, base, 0.0) if bi == bj else base
                n = same(own_id[bi], own_id[bj], float(BLK * (bi - bj)))
                return (scores * (table * decay(rate, n))).astype(BF16)

            for low_block in (0, 2):
                first = low_block * BLK
                scores = dot(queries[first:], keys[first : first + 256], 1, 1)
                weights = jnp.concatenate(
                    [
                        jnp.concatenate(
                            [
                                weigh(
                                    scores[bi * BLK - first : bi * BLK - first + BLK, j * BLK : j * BLK + BLK],
                                    bi, low_block + j,
                                )
                                for j in range(2)
                            ],
                            axis=1,
                        )
                        for bi in range(low_block, 4)
                    ],
                    axis=0,
                )
                part = dot(weights, values[first : first + 256], 1, 0)
                if low_block == 0:
                    total = part
            inner[h, :256, :] = total[:256]
            inner[h, 256:, :] = total[256:] + part
            gate = g[:, cols(h)].astype(F32)
            gated[h] = gain[:, cols(h)] * (gate / (1.0 + jnp.exp(-gate)))

    def remote(src, dst, send, recv, to):
        return pltpu.make_async_remote_copy(
            src_ref=src, dst_ref=dst, send_sem=send, recv_sem=recv, device_id=to, device_id_type=MESH_ID
        )

    SLOTS = ((1, 0), (1, 1), (3, 1), (3, 0), (1, 0), (3, 1))

    def phase_of(group):
        return min(group, 2)

    def piece(colour, group, coord, half):
        low, wide, order = COLOURS[colour]
        phase = phase_of(group)
        index = list(at) + [c]
        lanes = slice(low, low + wide)
        index[order[0]] = slice(0, 4) if half is None else slice(2 * half, 2 * half + 2)
        if phase == 2:
            index[order[1]] = near(order[1], group - 2)
        index[order[phase]] = coord
        return tuple(index) + (slice(None), lanes)

    started = []

    def ring_copy(colour, group, slot, step, coord, half):
        axis = COLOURS[colour][2][phase_of(group)]
        where = piece(colour, group, coord, half)
        return remote(
            w_all.at[where], w_all.at[where], w_send.at[colour, group, slot], w_recv.at[colour, group, slot],
            {names[axis]: near(axis, step)},
        )

    def direct_copy(colour, step, coord):
        low, wide, order = COLOURS[colour]
        index = list(at) + [c]
        index[order[0]] = coord
        return remote(
            w_all.at[x, y, z, c, :, low : low + wide],
            w_all.at[tuple(index) + (slice(None), slice(low, low + wide))],
            w_send.at[colour, 0, step], w_recv.at[colour, 0, step], {names[order[0]]: near(order[0], step)},
        )

    def line_start():
        for colour in range(3):
            for step in (1, 3, 2):
                copy = direct_copy(colour, step, at[COLOURS[colour][2][0]])
                copy.start()
                started.append(copy)

    def line_end():
        for colour in range(3):
            axis = COLOURS[colour][2][0]
            for step in (1, 3, 2):
                direct_copy(colour, step, near(axis, 4 - step)).wait_recv()
        for colour in range(3):
            twin(piece(colour, 1, at[COLOURS[colour][2][1]], None), 18 * colour)

    def ring_start(group):
        for colour in range(3):
            mine = at[COLOURS[colour][2][phase_of(group)]]
            for slot in (0, 2, 1, 3):
                step, half = SLOTS[slot]
                copy = ring_copy(colour, group, slot, step, mine, half)
                copy.start()
                started.append(copy)

    def ring_pass(group):
        for colour in range(3):
            axis = COLOURS[colour][2][phase_of(group)]
            for slot in (0, 2):
                step, half = SLOTS[slot]
                from_coord = near(axis, 4 - step)
                ring_copy(colour, group, slot, step, from_coord, half).wait_recv()
                copy = ring_copy(colour, group, 4 if slot == 0 else 5, step, from_coord, half)
                copy.start()
                started.append(copy)

    twins = []

    def twin(where, slot):
        copy = remote(w_all.at[where], w_all.at[where], b_send.at[slot], b_recv.at[slot], {C: 1 - c})
        copy.start()
        started.append(copy)
        twins.append((where[:3] + (1 - c,) + where[4:], slot))

    def ring_near(group):
        for colour in range(3):
            axis = COLOURS[colour][2][phase_of(group)]
            for slot in (1, 3):
                step, half = SLOTS[slot]
                ring_copy(colour, group, slot, step, near(axis, 4 - step), half).wait_recv()
            twin(piece(colour, group, near(axis, 1), None), 18 * colour + 3 * group)
            twin(piece(colour, group, near(axis, 3), None), 18 * colour + 3 * group + 1)

    def ring_far(group):
        for colour in range(3):
            axis = COLOURS[colour][2][phase_of(group)]
            for slot in (4, 5):
                step, half = SLOTS[slot]
                ring_copy(colour, group, slot, step, near(axis, 2), half).wait_recv()
            twin(piece(colour, group, near(axis, 2), None), 18 * colour + 3 * group + 2)

    def twin_waits():
        for where, slot in twins:
            view = w_all.at[where]
            remote(view, view, b_send.at[slot], b_recv.at[slot], {C: 1 - c}).wait_recv()

    pl.semaphore_wait(barrier, 10)
    loads[0].wait()
    line_start()
    loads[1].wait()
    loads[2].wait()
    states(s_out, (1 - c) * 8)
    core_copy = remote(s_out, s_in, c_send, c_recv, {C: 1 - c})
    core_copy.start()
    line_end()
    ring_start(1)
    states(s_own, c * 8)
    core_copy.wait()

    chip = z * 8
    n_first = jnp.where(c == 0, same(ids[chip + 3], ids[chip + 7], 512.0), 0.0)
    n_second = jnp.where(c == 1, same(ids[chip + 3], ids[chip + 7], 512.0), 0.0)
    for i in range(8):
        rate = rates[c * 8 + i]
        both = s_own[i] * decay(rate, n_first) + s_in[i] * decay(rate, n_second)
        z_out[i // 2, (i % 2) * DH : (i % 2) * DH + DH, :] = both.astype(BF16)

    def spread(copies):
        for copy in copies:
            copy.start()
        return copies

    def settle(copies):
        for copy in copies:
            copy.wait()

    line_copies = spread([
        remote(
            z_out.at[near(2, step)], z_in.at[3 - step], z_send.at[step - 1], z_recv.at[3 - step],
            {Z: near(2, step)},
        )
        for step in (1, 3, 2)
    ])
    loads[3].wait()
    loads[4].wait()
    loads[7].wait()
    ring_pass(1)
    ring_near(1)
    ring_start(3)
    attend(0, 3)
    ring_start(5)
    attend(3, 5)
    settle(line_copies)

    two = [rates[c * 8 + z * 2 + j] for j in range(2)]
    spots = [near(2, step) for step in range(4)]
    line_first, line_last = ids[0], ids[31]
    halves = (slice(0, DH), slice(DH, 2 * DH))

    def held(step, j):
        block = z_out[z, halves[j], :] if step == 0 else z_in[step - 1, halves[j], :]
        return block.astype(F32)

    for j, out in enumerate((y_out, x_out)):
        total = None
        for step in range(4):
            spot = spots[step]
            n = same(ids[spot * 8 + 7], line_last, (1024 * (3 - spot)).astype(F32))
            term = held(step, j) * decay(two[j], n)
            total = term if total is None else total + term
        out[:DH, :] = total.astype(BF16)
        note_row = lax.broadcasted_iota(jnp.int32, (16, DH), 0)
        notes = jnp.where(note_row < 8, line_last.astype(F32), line_first.astype(F32))
        out[DH : DH + 16, :] = notes.astype(BF16)
    column_copies = spread(
        [
            remote(
                src, into.at[3 - step], send.at[step - 1], recv.at[3 - step],
                {names[axis]: near(axis, step)},
            )
            for step in (1, 3, 2)
            for axis, src, into, send, recv in (
                (1, y_out, y_in, y_send, y_recv), (0, x_out, x_in, x_send, x_recv),
            )
        ]
    )
    for t in range(4):
        target = spots[t]
        for j in range(2):
            total = None
            for step in range(4):
                if step == t:
                    continue
                spot = spots[step]
                n = same(ids[spot * 8 + 7], ids[target * 8], (1024 * (target - 1 - spot)).astype(F32))
                term = held(step, j) * decay(two[j], jnp.where(spot < target, n, FAR))
                total = term if total is None else total + term
            p_part[t, halves[j], :] = total
    ring_pass(3)
    ring_far(1)
    ring_start(4)
    attend(5, 8)
    settle(column_copies)

    spots_y = [near(1, step) for step in range(4)]
    spots_x = [near(0, step) for step in range(4)]

    def view(own, came, step):
        return own if step == 0 else came.at[step - 1]

    def body_of(ref):
        return ref[:DH, :].astype(F32)

    def last_of(ref):
        return ref[DH : DH + 1, :].astype(F32)

    def first_of(ref):
        return ref[DH + 8 : DH + 9, :].astype(F32)

    by_y = [view(y_out, y_in, step) for step in range(4)]
    by_x = [view(x_out, x_in, step) for step in range(4)]
    slab_last = jnp.zeros((1, DH), F32)
    for step in range(4):
        slab_last = slab_last + jnp.where(spots_y[step] == 3, 1.0, 0.0) * last_of(by_y[step])
    total = None
    for step in range(4):
        spot = spots_y[step]
        n = same(last_of(by_y[step]), slab_last, (4096 * (3 - spot)).astype(F32))
        term = body_of(by_y[step]) * decay(two[0], n)
        total = term if total is None else total + term
    u_out[:DH, :] = total.astype(BF16)
    u_out[DH : DH + 16, :] = jnp.broadcast_to(slab_last, (16, DH)).astype(BF16)
    for t in range(4):
        target, first = spots_y[t], first_of(by_y[t])
        total = None
        for step in range(4):
            ref = by_x[step]
            if step == 0:
                n = same(last_of(ref), first, (4096 * (target - 1 - y)).astype(F32))
                n = jnp.where(y < target, n, FAR)
            else:
                spot = spots_x[step]
                lines = 4 * (x - spot) - y - 1 + target
                n = same(last_of(ref), first, (4096 * lines).astype(F32))
                n = jnp.where(spot < x, n, FAR)
            term = body_of(ref) * decay(two[1], n)
            total = term if total is None else total + term
        m_out[t] = total.astype(BF16)
    slab_copies = spread(
        [
            copy
            for step in (1, 3, 2)
            for copy in (
                remote(
                    u_out, u_in.at[3 - step], u_send.at[step - 1], u_recv.at[3 - step],
                    {X: near(0, step)},
                ),
                remote(
                    m_out.at[step], m_in.at[3 - step], m_send.at[step - 1], m_recv.at[3 - step],
                    {Y: near(1, step)},
                ),
            )
        ]
    )
    ring_pass(5)
    ring_start(2)
    attend(8, 9)
    ring_pass(4)
    attend(9, 11)
    settle(slab_copies)

    total = jnp.zeros((DH, DH), F32)
    first = line_first.astype(F32)
    for step in range(1, 4):
        ref, spot = by_y[step], spots_y[step]
        n = same(last_of(ref), first, (4096 * (y - 1 - spot)).astype(F32))
        total = total + body_of(ref) * decay(two[0], jnp.where(spot < y, n, FAR))
        ref, spot = u_in.at[step - 1], spots_x[step]
        n = same(last_of(ref), first, (16384 * (x - 1 - spot) + 4096 * y).astype(F32))
        total = total + body_of(ref) * decay(two[0], jnp.where(spot < x, n, FAR))
    fronts = [total]
    total = m_out[0].astype(F32)
    for step in range(3):
        total = total + m_in[step].astype(F32)
    fronts.append(total)
    for t in range(4):
        n = same(line_first, ids[spots[t] * 8], (1024 * spots[t]).astype(F32))
        for j in range(2):
            whole = p_part[t, halves[j], :] + fronts[j] * decay(two[j], n)
            p_out[t, halves[j], :] = whole.astype(BF16)
    back_copies = spread([
        remote(
            p_out.at[step], p_in.at[3 - step], p_send.at[step - 1], p_recv.at[3 - step],
            {Z: near(2, step)},
        )
        for step in (1, 3, 2)
    ])
    ring_near(3)
    ring_far(3)
    ring_near(5)
    ring_far(5)
    attend(11, 12)
    ring_pass(2)
    attend(12, 14)
    ring_near(4)
    ring_far(4)
    attend(14, 16)
    settle(back_copies)

    n_chip = same(ids[chip], ids[chip + 4], 512.0)
    n_core = same(ids[chip + 3], ids[chip + 4], 0.0)
    mine = jnp.where(c == 1, n_core, FAR)
    theirs = jnp.where(c == 0, n_core, FAR)
    for step in range(4):
        for j in range(2):
            i = spots[step] * 2 + j
            rate = rates[c * 8 + i]
            before = (p_out[0, halves[j], :] if step == 0 else p_in[step - 1, halves[j], :]).astype(F32)
            own = before * decay(rate, jnp.where(c == 1, n_chip, 0.0)) + s_in[i] * decay(rate, mine)
            away = before * decay(rate, jnp.where(c == 0, n_chip, 0.0)) + s_own[i] * decay(rate, theirs)
            p_own[i] = own.astype(BF16)
            c_out[i] = away.astype(BF16)
    pair_copy = remote(c_out, c_in, d_send, d_recv, {C: 1 - c})
    pair_copy.start()
    ring_near(2)
    ring_far(2)

    def finish(first, ref):
        @pl.loop(0, 8, unroll=4)
        def _(i):
            h = first + i
            carried = dot(q[:, cols(h)], ref[i], 1, 0)
            base = jnp.exp(-rates[h] * (row.astype(F32) + 1.0))
            for b in range(4):
                part = slice(b * BLK, b * BLK + BLK)
                reach = base * decay(rates[h], same(own_id[b], own_id[0], float(b * BLK)))
                mixed = (inner[h, part, :] + carried[part] * reach).astype(BF16).astype(F32)
                inv = lax.rsqrt(jnp.mean(mixed * mixed, axis=-1, keepdims=True) + 1e-06)
                nrm[part, cols(h)] = (mixed * inv * gated[h, part, :]).astype(BF16)

    finish(c * 8, p_own)
    pair_copy.wait()
    finish((1 - c) * 8, c_in)
    twin_waits()

    @pl.loop(0, 4)
    def _(n):
        lanes = pl.ds(pl.multiple_of(n * 512, 512), 512)
        weight = w_all[:, :, :, :, :, lanes].reshape(2048, 512)
        mixed_out[:, lanes] = dot(nrm[...], weight, 1, 0).astype(BF16)

    for copy in started:
        copy.wait_send()


def gather_and_attend(ids, rates, q, k, v, g, gain, w):
    tokens, width = q.shape
    heads = rates.shape[0]
    hbm = pl.BlockSpec(memory_space=pltpu.HBM)
    smem = pl.BlockSpec(memory_space=pltpu.SMEM)
    vmem = pltpu.VMEM
    dma = pltpu.SemaphoreType.DMA
    rows = w.shape[0]
    return pl.pallas_call(
        scan_kernel,
        out_shape=jax.ShapeDtypeStruct((tokens, width), BF16),
        in_specs=[hbm] * 8,
        out_specs=pl.BlockSpec(memory_space=vmem),
        scratch_shapes=[
            pltpu.SMEM((32,), jnp.int32),
            pltpu.SMEM((16,), F32),
            vmem((1, width), F32),
            vmem((tokens, width), BF16),
            vmem((tokens, width), BF16),
            vmem((tokens, width), BF16),
            vmem((tokens, width), BF16),
            vmem((4, 4, 4, 2, rows, width), BF16),
            vmem((tokens, width), BF16),
            vmem((heads, tokens, DH), F32),
            vmem((heads, tokens, DH), F32),
            vmem((512, DH), F32),
            vmem((512, DH), BF16),
            vmem((8, DH, DH), F32),
            vmem((8, DH, DH), F32),
            vmem((8, DH, DH), F32),
            vmem((4, 2 * DH, DH), BF16),
            vmem((3, 2 * DH, DH), BF16),
            vmem((4, 2 * DH, DH), F32),
            vmem((DH + 16, DH), BF16),
            vmem((3, DH + 16, DH), BF16),
            vmem((DH + 16, DH), BF16),
            vmem((3, DH + 16, DH), BF16),
            vmem((DH + 16, DH), BF16),
            vmem((3, DH + 16, DH), BF16),
            vmem((4, DH, DH), BF16),
            vmem((3, DH, DH), BF16),
            vmem((4, 2 * DH, DH), BF16),
            vmem((3, 2 * DH, DH), BF16),
            vmem((8, DH, DH), BF16),
            vmem((8, DH, DH), BF16),
            vmem((8, DH, DH), BF16),
            dma((8,)),
            dma, dma,
            dma((3,)), dma((3,)),
            dma((3,)), dma((3,)),
            dma((3,)), dma((3,)),
            dma((3,)), dma((3,)),
            dma((3,)), dma((3,)),
            dma((3,)), dma((3,)),
            dma, dma,
            dma((3, 6, 6)), dma((3, 6, 6)),
            dma((54,)), dma((54,)),
        ],
        compiler_params=pltpu.CompilerParams(
            collective_id=0, has_side_effects=True, vmem_limit_bytes=48 << 20
        ),
        name="scan_and_gather",
    )(*(pltpu.with_memory_space_constraint(a, pltpu.HBM) for a in (ids, rates, q, k, v, g, gain, w)))


def on_device(query_rows, key_rows, value_rows, gate_rows, segment_ids, decay_rates, norm_gain, out_weight):
    width = query_rows.shape[1]
    return gather_and_attend(
        segment_ids, decay_rates, query_rows, key_rows, value_rows, gate_rows,
        norm_gain.reshape(1, width), out_weight,
    )


def solution(mesh):
    split = Mesh(mesh.devices.reshape(4, 4, 4, 2), SEQ_HEAD)
    rows = P(SEQ_HEAD, None)
    return jax.shard_map(
        on_device,
        mesh=split,
        in_specs=(rows, rows, rows, rows, P(SEQ), P(), P(), rows),
        out_specs=rows,
        check_vma=False,
    )
```

```python
import functools

import jax
import jax.numpy as jnp
from jax import lax
from jax.experimental import pallas as pl
from jax.experimental.pallas import tpu as pltpu
from jax.sharding import Mesh
from jax.sharding import PartitionSpec as P

BLK = 128
SBLK = 512
DH = 128
FAR = 1e30
X, Y, Z, C = "seq_0", "seq_1", "head_0", "head_1"
SEQ_HEAD = (X, Y, Z, C)
SEQ = (X, Y)
MESH_ID = pl.DeviceIdType.MESH
F32, BF16 = jnp.float32, jnp.bfloat16

COLOURS = (
    (0, 768, (2, 1, 0)),
    (768, 512, (1, 0, 2)),
    (1280, 768, (0, 2, 1)),
)


def dot(a, b, ca, cb):
    return lax.dot_general(a, b, (((ca,), (cb,)), ((), ())), preferred_element_type=F32)


def same(a, b, n):
    return jnp.where(a == b, n, FAR)


def decay(rate, n):
    return jnp.exp(-rate * jnp.broadcast_to(n, (1, DH)))


def scan_kernel(
    ids_hbm, rates_hbm, q_hbm, k_hbm, v_hbm, g_hbm, gain_hbm, w_in,
    mixed_out,
    ids, rates, gain, q, k, v, g, w_all, nrm, inner, gated, keep_n, lasting,
    s_own, s_out, s_in, z_out, z_in, p_part, y_out, y_in, x_out, x_in, u_out, u_in, m_out, m_in,
    p_out, p_in, c_out, c_in, p_own,
    load_sem, c_send, c_recv, z_send, z_recv, y_send, y_recv, x_send, x_recv,
    u_send, u_recv, m_send, m_recv, p_send, p_recv, d_send, d_recv, w_send, w_recv, b_send, b_recv,
):
    at = (lax.axis_index(X), lax.axis_index(Y), lax.axis_index(Z))
    x, y, z = at
    c = lax.axis_index(C)
    names = (X, Y, Z)

    def near(axis, step):
        return lax.rem(at[axis] + step, 4)

    barrier = pltpu.get_barrier_semaphore()
    pl.semaphore_signal(barrier, inc=1, device_id={C: 1 - c}, device_id_type=MESH_ID)
    for axis in range(3):
        for step in (1, 2, 3):
            pl.semaphore_signal(
                barrier, inc=1, device_id={names[axis]: near(axis, step)}, device_id_type=MESH_ID
            )
    loads = [
        pltpu.make_async_copy(src, dst, load_sem.at[n])
        for n, (src, dst) in enumerate(
            ((w_in, w_all.at[x, y, z, c]), (k_hbm, k), (v_hbm, v), (q_hbm, q), (g_hbm, g),
             (ids_hbm, ids), (rates_hbm, rates), (gain_hbm, gain))
        )
    ]
    for n in (5, 6, 0, 1, 2, 3, 4, 7):
        loads[n].start()
    loads[5].wait()
    loads[6].wait()

    place = z * 2 + c
    own_id = [ids[place * 4 + b] for b in range(4)]
    row = lax.broadcasted_iota(jnp.int32, (BLK, BLK), 0)
    column = lax.broadcasted_iota(jnp.int32, (BLK, BLK), 1)
    for b in range(4):
        part = slice(b * BLK, b * BLK + BLK)
        keep_n[part, :] = (SBLK - 1.0 - b * BLK) - row.astype(F32) + same(own_id[b], own_id[3], 0.0)
        last = jnp.where(own_id[b] == own_id[3], 1.0, 0.0)
        lasting[part, :] = jnp.full((BLK, DH), last, F32).astype(BF16)

    def cols(h):
        return pl.ds(pl.multiple_of(h * DH, DH), DH)

    def states(into, first):
        @pl.loop(0, 8, unroll=4)
        def _(i):
            h = first + i
            values = v[:, cols(h)]
            lost = lasting[...].astype(F32) - jnp.exp(-rates[h] * keep_n[...])
            pair = jnp.concatenate([values * lasting[...], values * lost.astype(BF16)], axis=1)
            both = dot(k[:, cols(h)], pair, 0, 0)
            into[i] = both[:, :DH] - both[:, DH:]

    def attend(low, high):
        @pl.loop(low, high)
        def _(h):
            rate = rates[h]
            queries, keys, values = q[:, cols(h)], k[:, cols(h)], v[:, cols(h)]
            ahead = row - column
            base = jnp.exp(-rate * ahead.astype(F32))

            def weigh(scores, bi, bj):
                if bj > bi:
                    return jnp.zeros((BLK, BLK), BF16)
                table = jnp.where(ahead >= 0, base, 0.0) if bi == bj else base
                n = same(own_id[bi], own_id[bj], float(BLK * (bi - bj)))
                return (scores * (table * decay(rate, n))).astype(BF16)

            for low_block in (0, 2):
                first = low_block * BLK
                scores = dot(queries[first:], keys[first : first + 256], 1, 1)
                weights = jnp.concatenate(
                    [
                        jnp.concatenate(
                            [
                                weigh(
                                    scores[bi * BLK - first : bi * BLK - first + BLK, j * BLK : j * BLK + BLK],
                                    bi, low_block + j,
                                )
                                for j in range(2)
                            ],
                            axis=1,
                        )
                        for bi in range(low_block, 4)
                    ],
                    axis=0,
                )
                part = dot(weights, values[first : first + 256], 1, 0)
                if low_block == 0:
                    total = part
            inner[h, :256, :] = total[:256]
            inner[h, 256:, :] = total[256:] + part
            gate = g[:, cols(h)].astype(F32)
            gated[h] = gain[:, cols(h)] * (gate / (1.0 + jnp.exp(-gate)))

    def remote(src, dst, send, recv, to):
        return pltpu.make_async_remote_copy(
            src_ref=src, dst_ref=dst, send_sem=send, recv_sem=recv, device_id=to, device_id_type=MESH_ID
        )

    SLOTS = ((1, 0), (1, 1), (3, 1), (3, 0), (1, 0), (3, 1))

    def phase_of(group):
        return min(group, 2)

    def piece(colour, group, coord, half):
        low, wide, order = COLOURS[colour]
        phase = phase_of(group)
        index = list(at) + [c]
        lanes = slice(low, low + wide)
        index[order[0]] = slice(0, 4) if half is None else slice(2 * half, 2 * half + 2)
        if phase == 2:
            index[order[1]] = near(order[1], group - 2)
        index[order[phase]] = coord
        return tuple(index) + (slice(None), lanes)

    started = []

    def ring_copy(colour, group, slot, step, coord, half):
        axis = COLOURS[colour][2][phase_of(group)]
        where = piece(colour, group, coord, half)
        return remote(
            w_all.at[where], w_all.at[where], w_send.at[colour, group, slot], w_recv.at[colour, group, slot],
            {names[axis]: near(axis, step)},
        )

    def direct_copy(colour, step, coord):
        low, wide, order = COLOURS[colour]
        index = list(at) + [c]
        index[order[0]] = coord
        return remote(
            w_all.at[x, y, z, c, :, low : low + wide],
            w_all.at[tuple(index) + (slice(None), slice(low, low + wide))],
            w_send.at[colour, 0, step], w_recv.at[colour, 0, step], {names[order[0]]: near(order[0], step)},
        )

    def line_start():
        for colour in range(3):
            for step in (1, 3, 2):
                copy = direct_copy(colour, step, at[COLOURS[colour][2][0]])
                copy.start()
                started.append(copy)

    def line_end():
        for colour in range(3):
            axis = COLOURS[colour][2][0]
            for step in (1, 3, 2):
                direct_copy(colour, step, near(axis, 4 - step)).wait_recv()
        for colour in range(3):
            twin(piece(colour, 1, at[COLOURS[colour][2][1]], None), 18 * colour)

    def ring_start(group):
        for colour in range(3):
            mine = at[COLOURS[colour][2][phase_of(group)]]
            for slot in (0, 2, 1, 3):
                step, half = SLOTS[slot]
                copy = ring_copy(colour, group, slot, step, mine, half)
                copy.start()
                started.append(copy)

    def ring_pass(group):
        for colour in range(3):
            axis = COLOURS[colour][2][phase_of(group)]
            for slot in (0, 2):
                step, half = SLOTS[slot]
                from_coord = near(axis, 4 - step)
                ring_copy(colour, group, slot, step, from_coord, half).wait_recv()
                copy = ring_copy(colour, group, 4 if slot == 0 else 5, step, from_coord, half)
                copy.start()
                started.append(copy)

    twins = []

    def twin(where, slot):
        copy = remote(w_all.at[where], w_all.at[where], b_send.at[slot], b_recv.at[slot], {C: 1 - c})
        copy.start()
        started.append(copy)
        twins.append((where[:3] + (1 - c,) + where[4:], slot))

    def ring_near(group):
        for colour in range(3):
            axis = COLOURS[colour][2][phase_of(group)]
            for slot in (1, 3):
                step, half = SLOTS[slot]
                ring_copy(colour, group, slot, step, near(axis, 4 - step), half).wait_recv()
            twin(piece(colour, group, near(axis, 1), None), 18 * colour + 3 * group)
            twin(piece(colour, group, near(axis, 3), None), 18 * colour + 3 * group + 1)

    def ring_far(group):
        for colour in range(3):
            axis = COLOURS[colour][2][phase_of(group)]
            for slot in (4, 5):
                step, half = SLOTS[slot]
                ring_copy(colour, group, slot, step, near(axis, 2), half).wait_recv()
            twin(piece(colour, group, near(axis, 2), None), 18 * colour + 3 * group + 2)

    def twin_waits():
        for where, slot in twins:
            view = w_all.at[where]
            remote(view, view, b_send.at[slot], b_recv.at[slot], {C: 1 - c}).wait_recv()

    pl.semaphore_wait(barrier, 10)
    loads[0].wait()
    line_start()
    loads[1].wait()
    loads[2].wait()
    states(s_out, (1 - c) * 8)
    core_copy = remote(s_out, s_in, c_send, c_recv, {C: 1 - c})
    core_copy.start()
    line_end()
    ring_start(1)
    states(s_own, c * 8)
    core_copy.wait()

    chip = z * 8
    n_first = jnp.where(c == 0, same(ids[chip + 3], ids[chip + 7], 512.0), 0.0)
    n_second = jnp.where(c == 1, same(ids[chip + 3], ids[chip + 7], 512.0), 0.0)
    for i in range(8):
        rate = rates[c * 8 + i]
        both = s_own[i] * decay(rate, n_first) + s_in[i] * decay(rate, n_second)
        z_out[i // 2, (i % 2) * DH : (i % 2) * DH + DH, :] = both.astype(BF16)

    def spread(copies):
        for copy in copies:
            copy.start()
        return copies

    def settle(copies):
        for copy in copies:
            copy.wait()

    line_copies = spread([
        remote(
            z_out.at[near(2, step)], z_in.at[3 - step], z_send.at[step - 1], z_recv.at[3 - step],
            {Z: near(2, step)},
        )
        for step in (1, 3, 2)
    ])
    loads[3].wait()
    loads[4].wait()
    loads[7].wait()
    ring_pass(1)
    ring_near(1)
    ring_start(3)
    attend(0, 3)
    ring_start(5)
    attend(3, 5)
    settle(line_copies)

    two = [rates[c * 8 + z * 2 + j] for j in range(2)]
    spots = [near(2, step) for step in range(4)]
    line_first, line_last = ids[0], ids[31]
    halves = (slice(0, DH), slice(DH, 2 * DH))

    def held(step, j):
        block = z_out[z, halves[j], :] if step == 0 else z_in[step - 1, halves[j], :]
        return block.astype(F32)

    for j, out in enumerate((y_out, x_out)):
        total = None
        for step in range(4):
            spot = spots[step]
            n = same(ids[spot * 8 + 7], line_last, (1024 * (3 - spot)).astype(F32))
            term = held(step, j) * decay(two[j], n)
            total = term if total is None else total + term
        out[:DH, :] = total.astype(BF16)
        note_row = lax.broadcasted_iota(jnp.int32, (16, DH), 0)
        notes = jnp.where(note_row < 8, line_last.astype(F32), line_first.astype(F32))
        out[DH : DH + 16, :] = notes.astype(BF16)
    column_copies = spread(
        [
            remote(
                src, into.at[3 - step], send.at[step - 1], recv.at[3 - step],
                {names[axis]: near(axis, step)},
            )
            for step in (1, 3, 2)
            for axis, src, into, send, recv in (
                (1, y_out, y_in, y_send, y_recv), (0, x_out, x_in, x_send, x_recv),
            )
        ]
    )
    for t in range(4):
        target = spots[t]
        for j in range(2):
            total = None
            for step in range(4):
                if step == t:
                    continue
                spot = spots[step]
                n = same(ids[spot * 8 + 7], ids[target * 8], (1024 * (target - 1 - spot)).astype(F32))
                term = held(step, j) * decay(two[j], jnp.where(spot < target, n, FAR))
                total = term if total is None else total + term
            p_part[t, halves[j], :] = total
    ring_pass(3)
    ring_far(1)
    ring_start(4)
    attend(5, 8)
    settle(column_copies)

    spots_y = [near(1, step) for step in range(4)]
    spots_x = [near(0, step) for step in range(4)]

    def view(own, came, step):
        return own if step == 0 else came.at[step - 1]

    def body_of(ref):
        return ref[:DH, :].astype(F32)

    def last_of(ref):
        return ref[DH : DH + 1, :].astype(F32)

    def first_of(ref):
        return ref[DH + 8 : DH + 9, :].astype(F32)

    by_y = [view(y_out, y_in, step) for step in range(4)]
    by_x = [view(x_out, x_in, step) for step in range(4)]
    slab_last = jnp.zeros((1, DH), F32)
    for step in range(4):
        slab_last = slab_last + jnp.where(spots_y[step] == 3, 1.0, 0.0) * last_of(by_y[step])
    total = None
    for step in range(4):
        spot = spots_y[step]
        n = same(last_of(by_y[step]), slab_last, (4096 * (3 - spot)).astype(F32))
        term = body_of(by_y[step]) * decay(two[0], n)
        total = term if total is None else total + term
    u_out[:DH, :] = total.astype(BF16)
    u_out[DH : DH + 16, :] = jnp.broadcast_to(slab_last, (16, DH)).astype(BF16)
    for t in range(4):
        target, first = spots_y[t], first_of(by_y[t])
        total = None
        for step in range(4):
            ref = by_x[step]
            if step == 0:
                n = same(last_of(ref), first, (4096 * (target - 1 - y)).astype(F32))
                n = jnp.where(y < target, n, FAR)
            else:
                spot = spots_x[step]
                lines = 4 * (x - spot) - y - 1 + target
                n = same(last_of(ref), first, (4096 * lines).astype(F32))
                n = jnp.where(spot < x, n, FAR)
            term = body_of(ref) * decay(two[1], n)
            total = term if total is None else total + term
        m_out[t] = total.astype(BF16)
    slab_copies = spread(
        [
            copy
            for step in (1, 3, 2)
            for copy in (
                remote(
                    u_out, u_in.at[3 - step], u_send.at[step - 1], u_recv.at[3 - step],
                    {X: near(0, step)},
                ),
                remote(
                    m_out.at[step], m_in.at[3 - step], m_send.at[step - 1], m_recv.at[3 - step],
                    {Y: near(1, step)},
                ),
            )
        ]
    )
    ring_pass(5)
    ring_start(2)
    attend(8, 9)
    ring_pass(4)
    attend(9, 11)
    settle(slab_copies)

    total = jnp.zeros((DH, DH), F32)
    first = line_first.astype(F32)
    for step in range(1, 4):
        ref, spot = by_y[step], spots_y[step]
        n = same(last_of(ref), first, (4096 * (y - 1 - spot)).astype(F32))
        total = total + body_of(ref) * decay(two[0], jnp.where(spot < y, n, FAR))
        ref, spot = u_in.at[step - 1], spots_x[step]
        n = same(last_of(ref), first, (16384 * (x - 1 - spot) + 4096 * y).astype(F32))
        total = total + body_of(ref) * decay(two[0], jnp.where(spot < x, n, FAR))
    fronts = [total]
    total = m_out[0].astype(F32)
    for step in range(3):
        total = total + m_in[step].astype(F32)
    fronts.append(total)
    for t in range(4):
        n = same(line_first, ids[spots[t] * 8], (1024 * spots[t]).astype(F32))
        for j in range(2):
            whole = p_part[t, halves[j], :] + fronts[j] * decay(two[j], n)
            p_out[t, halves[j], :] = whole.astype(BF16)
    back_copies = spread([
        remote(
            p_out.at[step], p_in.at[3 - step], p_send.at[step - 1], p_recv.at[3 - step],
            {Z: near(2, step)},
        )
        for step in (1, 3, 2)
    ])
    ring_near(3)
    ring_far(3)
    ring_near(5)
    ring_far(5)
    attend(11, 12)
    ring_pass(2)
    attend(12, 14)
    ring_near(4)
    ring_far(4)
    attend(14, 16)
    settle(back_copies)

    n_chip = same(ids[chip], ids[chip + 4], 512.0)
    n_core = same(ids[chip + 3], ids[chip + 4], 0.0)
    mine = jnp.where(c == 1, n_core, FAR)
    theirs = jnp.where(c == 0, n_core, FAR)
    for step in range(4):
        for j in range(2):
            i = spots[step] * 2 + j
            rate = rates[c * 8 + i]
            before = (p_out[0, halves[j], :] if step == 0 else p_in[step - 1, halves[j], :]).astype(F32)
            own = before * decay(rate, jnp.where(c == 1, n_chip, 0.0)) + s_in[i] * decay(rate, mine)
            away = before * decay(rate, jnp.where(c == 0, n_chip, 0.0)) + s_own[i] * decay(rate, theirs)
            p_own[i] = own.astype(BF16)
            c_out[i] = away.astype(BF16)
    pair_copy = remote(c_out, c_in, d_send, d_recv, {C: 1 - c})
    pair_copy.start()
    ring_near(2)
    ring_far(2)

    def finish(first, ref):
        @pl.loop(0, 8, unroll=4)
        def _(i):
            h = first + i
            carried = dot(q[:, cols(h)], ref[i], 1, 0)
            base = jnp.exp(-rates[h] * (row.astype(F32) + 1.0))
            for b in range(4):
                part = slice(b * BLK, b * BLK + BLK)
                reach = base * decay(rates[h], same(own_id[b], own_id[0], float(b * BLK)))
                mixed = (inner[h, part, :] + carried[part] * reach).astype(BF16).astype(F32)
                inv = lax.rsqrt(jnp.mean(mixed * mixed, axis=-1, keepdims=True) + 1e-06)
                nrm[part, cols(h)] = (mixed * inv * gated[h, part, :]).astype(BF16)

    finish(c * 8, p_own)
    pair_copy.wait()
    finish((1 - c) * 8, c_in)
    twin_waits()

    @pl.loop(0, 4, unroll=2)
    def _(n):
        lanes = pl.ds(pl.multiple_of(n * 512, 512), 512)
        weight = w_all[:, :, :, :, :, lanes].reshape(2048, 512)
        mixed_out[:, lanes] = dot(nrm[...], weight, 1, 0).astype(BF16)

    for copy in started:
        copy.wait_send()


def gather_and_attend(ids, rates, q, k, v, g, gain, w):
    tokens, width = q.shape
    heads = rates.shape[0]
    hbm = pl.BlockSpec(memory_space=pltpu.HBM)
    smem = pl.BlockSpec(memory_space=pltpu.SMEM)
    vmem = pltpu.VMEM
    dma = pltpu.SemaphoreType.DMA
    rows = w.shape[0]
    return pl.pallas_call(
        scan_kernel,
        out_shape=jax.ShapeDtypeStruct((tokens, width), BF16),
        in_specs=[hbm] * 8,
        out_specs=pl.BlockSpec(memory_space=vmem),
        scratch_shapes=[
            pltpu.SMEM((32,), jnp.int32),
            pltpu.SMEM((16,), F32),
            vmem((1, width), F32),
            vmem((tokens, width), BF16),
            vmem((tokens, width), BF16),
            vmem((tokens, width), BF16),
            vmem((tokens, width), BF16),
            vmem((4, 4, 4, 2, rows, width), BF16),
            vmem((tokens, width), BF16),
            vmem((heads, tokens, DH), F32),
            vmem((heads, tokens, DH), F32),
            vmem((512, DH), F32),
            vmem((512, DH), BF16),
            vmem((8, DH, DH), F32),
            vmem((8, DH, DH), F32),
            vmem((8, DH, DH), F32),
            vmem((4, 2 * DH, DH), BF16),
            vmem((3, 2 * DH, DH), BF16),
            vmem((4, 2 * DH, DH), F32),
            vmem((DH + 16, DH), BF16),
            vmem((3, DH + 16, DH), BF16),
            vmem((DH + 16, DH), BF16),
            vmem((3, DH + 16, DH), BF16),
            vmem((DH + 16, DH), BF16),
            vmem((3, DH + 16, DH), BF16),
            vmem((4, DH, DH), BF16),
            vmem((3, DH, DH), BF16),
            vmem((4, 2 * DH, DH), BF16),
            vmem((3, 2 * DH, DH), BF16),
            vmem((8, DH, DH), BF16),
            vmem((8, DH, DH), BF16),
            vmem((8, DH, DH), BF16),
            dma((8,)),
            dma, dma,
            dma((3,)), dma((3,)),
            dma((3,)), dma((3,)),
            dma((3,)), dma((3,)),
            dma((3,)), dma((3,)),
            dma((3,)), dma((3,)),
            dma((3,)), dma((3,)),
            dma, dma,
            dma((3, 6, 6)), dma((3, 6, 6)),
            dma((54,)), dma((54,)),
        ],
        compiler_params=pltpu.CompilerParams(
            collective_id=0, has_side_effects=True, vmem_limit_bytes=48 << 20
        ),
        name="scan_and_gather",
    )(*(pltpu.with_memory_space_constraint(a, pltpu.HBM) for a in (ids, rates, q, k, v, g, gain, w)))


def on_device(query_rows, key_rows, value_rows, gate_rows, segment_ids, decay_rates, norm_gain, out_weight):
    width = query_rows.shape[1]
    return gather_and_attend(
        segment_ids, decay_rates, query_rows, key_rows, value_rows, gate_rows,
        norm_gain.reshape(1, width), out_weight,
    )


def solution(mesh):
    split = Mesh(mesh.devices.reshape(4, 4, 4, 2), SEQ_HEAD)
    rows = P(SEQ_HEAD, None)
    return jax.shard_map(
        on_device,
        mesh=split,
        in_specs=(rows, rows, rows, rows, P(SEQ), P(), P(), rows),
        out_specs=rows,
        check_vma=False,
    )
```
